32 devices in a mesh: depth: 4 (over y, core), row: 4 (over z), col: 2 (over x).
Axes of the slice: x: 2, y: 2, z: 4, core: 2. Of those that a mesh axis runs over, the one named last changes fastest.
Arguments:
- left_factor: bfloat16 [1792, 32, 512], P('depth', None, 'row'), may hold values from -6 to 6
- right_factor: bfloat16 [1792, 32, 512], P('depth', None, 'col'), may hold values from -6 to 6
- out_weight: bfloat16 [1024, 128], replicated, may hold values from -12 to 12
- pair_cotangent: bfloat16 [512, 512, 128], P(('row', 'depth'), 'col'), may hold values from -0.29882812 to 0.29882812
Outputs:
- left_grad: float32 [1792, 32, 512], P(('depth', 'col'), None, 'row')
- right_grad: float32 [1792, 32, 512], P(('depth', 'row'), None, 'col')
- weight_grad: float32 [1024, 128], P(('depth', 'row', 'col'))
The draws below stay inside these ranges and needn't reach their ends.
All inputs are finite; a program needn't handle non-finite values.
Results may differ from the reference program's by a relative error of at most 0.0075.
Values may be sent and summed in bfloat16 or wider, within the bound.
A program may use at most 320 MiB of HBM per device.

```python
import jax
import jax.numpy as jnp
from jax import lax

C = 32
P_SIZE = 128
TOK_ROW = 128
CC = 1024
S = 1792
N = 512


def block_scale(rng, dims, split, smallest, largest):
    gain = 1.0
    for axis_at, blocks in split:
        heights = jax.random.uniform(jax.random.fold_in(jax.random.fold_in(rng, 6), axis_at), (blocks,), jnp.float32, smallest / len(split), largest / len(split))
        gain = gain * jnp.repeat(jnp.exp(heights), dims[axis_at] // blocks).reshape((-1,) + (1,) * (len(dims) - 1 - axis_at))
    return gain


def bell_draw(key, shape, deviation, reach, shards=(), kind=jnp.bfloat16):
    factor_of = block_scale(key, shape, shards, -0.22, 0.18) if shards else 1.0
    entries = jax.random.normal(key, shape, jnp.float32) * deviation * factor_of
    return jnp.minimum(jnp.maximum(entries, -reach), reach).astype(kind)


def setup_inputs(seed: int = 0) -> dict:
    seeds = jax.random.split(jax.random.key(seed), 5)
    return {
        "left_factor": bell_draw(seeds[0], (S, C, N), 1.0, 6.0, ((0, 4), (2, 4))),
        "right_factor": bell_draw(seeds[1], (S, C, N), 1.0, 6.0, ((0, 4), (2, 2))),
        "out_weight": bell_draw(seeds[2], (CC, P_SIZE), 2.0, 12.0),
        "pair_cotangent": bell_draw(seeds[3], (N, N, P_SIZE), 0.05, 0.29882812, ((0, 16), (1, 2))),
    }


def reference(left_factor, right_factor, out_weight, pair_cotangent):
    seq_total = left_factor.shape[0]
    left_f = left_factor.astype(jnp.float32)
    right_f = right_factor.astype(jnp.float32)
    width = out_weight.shape[0]
    chans = left_factor.shape[1]
    pair_ch = out_weight.shape[1]
    tokens = left_factor.shape[2]
    blocks = tokens // TOK_ROW
    high = lax.Precision.HIGHEST

    def step(carry, block):
        wsum, rsum = carry
        first_row = (block * TOK_ROW).astype(jnp.int32)
        left_blk = lax.dynamic_slice_in_dim(left_f, first_row, TOK_ROW, 2)
        grad_blk = lax.dynamic_slice_in_dim(pair_cotangent, first_row, TOK_ROW, 0)
        outer = jnp.einsum('sci,sej->ijce', left_blk, right_f, precision=high) / seq_total
        outer = outer.reshape(TOK_ROW * tokens, width).astype(jnp.bfloat16)
        grad_two = grad_blk.reshape(TOK_ROW * tokens, pair_ch)
        delta = jnp.dot(grad_two, out_weight.T, preferred_element_type=jnp.float32).astype(jnp.bfloat16)
        wsum = wsum + jnp.dot(outer.T, grad_two, preferred_element_type=jnp.float32)
        delta_four = delta.astype(jnp.float32).reshape(TOK_ROW, tokens, chans, chans)
        left_blk_grad = jnp.einsum('ijce,sej->sci', delta_four, right_f, precision=high) / seq_total
        rsum = rsum + jnp.einsum('ijce,sci->sej', delta_four, left_blk, precision=high) / seq_total
        return (wsum, rsum), left_blk_grad

    start = (jnp.zeros((width, pair_ch), jnp.float32), jnp.zeros(right_f.shape, jnp.float32))
    (weight_grad, right_grad), pieces = lax.scan(step, start, jnp.arange(blocks, dtype=jnp.int32))
    left_grad = jnp.transpose(pieces, (1, 2, 0, 3)).reshape(seq_total, chans, tokens)
    return left_grad, right_grad, weight_grad
```

```python
import functools

import jax
import jax.numpy as jnp
from jax import lax
from jax.experimental import pallas as pl
from jax.experimental.pallas import tpu as pltpu
from jax.sharding import PartitionSpec as P

F32 = jnp.float32
BF16 = jnp.bfloat16
VMEM_CAP = 60 * 1024 * 1024
MEGA_VMEM = 62 * 1024 * 1024
MESH = pl.DeviceIdType.MESH


def params():
    return pltpu.CompilerParams(vmem_limit_bytes=VMEM_CAP)


def cost(flops, nbytes):
    return pl.CostEstimate(flops=flops, bytes_accessed=nbytes, transcendentals=0)


def outer_kernel(inv, at_ref, b_ref, o_ref):
    width = 512 if o_ref.shape[1] % 512 == 0 else o_ref.shape[1]
    for n in range(o_ref.shape[1] // width):
        cols = slice(n * width, (n + 1) * width)
        acc = jnp.dot(at_ref[...], b_ref[:, cols], preferred_element_type=F32)
        o_ref[:, cols] = (acc * inv).astype(BF16)


def outer_call(at, b2, inv, tm, tn, part, cols):
    rows, seqs = at.shape
    first = part * cols // tn
    return pl.pallas_call(
        functools.partial(outer_kernel, inv),
        out_shape=jax.ShapeDtypeStruct((rows, cols), BF16),
        grid=(cols // tn, rows // tm),
        in_specs=[
            pl.BlockSpec((tm, seqs), lambda n, m: (m, 0)),
            pl.BlockSpec((seqs, tn), lambda n, m: (0, n + first)),
        ],
        out_specs=pl.BlockSpec((tm, tn), lambda n, m: (m, n)),
        compiler_params=params(),
        cost_estimate=cost(2 * rows * cols * seqs, 2 * rows * cols + 2 * seqs * (rows + cols)),
        name=f"outer_{part}",
    )(at, b2)


def delta_kernel(inv, chans, toks, w_ref, g_ref, a_ref, d_ref, r_ref, acc_ref):
    step = pl.program_id(0)
    here = g_ref.shape[0]
    eb = w_ref.shape[0] // chans

    def one(i, carry):
        d = lax.dot_general(
            w_ref[...], g_ref[i], (((1,), (1,)), ((), ())), preferred_element_type=F32
        ).astype(BF16)
        at = pl.multiple_of(i * chans, chans)
        for e in range(eb):
            d_ref[pl.ds(at, chans), e * toks:(e + 1) * toks] = d[e * chans:(e + 1) * chans]
        return carry

    lax.fori_loop(0, here, one, 0, unroll=8)

    @pl.when(step == 0)
    def _():
        acc_ref[...] = jnp.zeros_like(acc_ref)

    for e in range(eb):
        cols = slice(e * toks, (e + 1) * toks)
        acc_ref[:, cols] += jnp.dot(a_ref[...], d_ref[:, cols], preferred_element_type=F32)

    @pl.when(step == pl.num_programs(0) - 1)
    def _():
        r_ref[...] = (acc_ref[...] * inv).astype(BF16)


def delta_call(w_ec, g, a2, inv, chans, part, eb, ti):
    rows, toks, pair_ch = g.shape
    seqs = a2.shape[0]
    wide = eb * toks
    return pl.pallas_call(
        functools.partial(delta_kernel, inv, chans, toks),
        out_shape=(
            jax.ShapeDtypeStruct((rows * chans, wide), BF16),
            jax.ShapeDtypeStruct((seqs, wide), BF16),
        ),
        grid=(rows // ti,),
        in_specs=[
            pl.BlockSpec((eb * chans, pair_ch), lambda m: (part, 0)),
            pl.BlockSpec((ti, toks, pair_ch), lambda m: (m, 0, 0)),
            pl.BlockSpec((seqs, ti * chans), lambda m: (0, m)),
        ],
        out_specs=(
            pl.BlockSpec((ti * chans, wide), lambda m: (m, 0)),
            pl.BlockSpec((seqs, wide), lambda m: (0, 0)),
        ),
        scratch_shapes=[pltpu.VMEM((seqs, wide), F32)],
        compiler_params=params(),
        cost_estimate=cost(
            2 * rows * chans * wide * (seqs + 2 * pair_ch),
            2 * rows * (chans * wide + toks * pair_ch + chans * seqs),
        ),
        name=f"delta_right_{part}",
    )(w_ec, g, a2)


def left_kernel(inv, parts, b_ref, *refs):
    d_refs, o_ref = refs[:parts], refs[parts]
    wide = d_refs[0].shape[1]
    acc = None
    for k in range(parts):
        term = lax.dot_general(
            b_ref[:, k * wide:(k + 1) * wide],
            d_refs[k][...],
            (((1,), (1,)), ((), ())),
            preferred_element_type=F32,
        )
        acc = term if acc is None else acc + term
    o_ref[...] = (acc * inv).astype(BF16)


def left_call(b2, ds, inv, tn):
    seqs = b2.shape[0]
    rows, wide = ds[0].shape
    parts = len(ds)
    return pl.pallas_call(
        functools.partial(left_kernel, inv, parts),
        out_shape=jax.ShapeDtypeStruct((seqs, rows), BF16),
        grid=(rows // tn,),
        in_specs=[pl.BlockSpec((seqs, parts * wide), lambda m: (0, 0))]
        + [pl.BlockSpec((tn, wide), lambda m: (m, 0))] * parts,
        out_specs=pl.BlockSpec((seqs, tn), lambda m: (0, m)),
        compiler_params=params(),
        cost_estimate=cost(2 * seqs * rows * wide * parts, 2 * rows * wide * parts + 4 * seqs * rows),
        name="left",
    )(b2, *ds)


def weight_kernel(chans, *refs):
    o_refs, g_ref, w_ref = refs[:-2], refs[-2], refs[-1]
    ti, toks, pair_ch = g_ref.shape
    per = o_refs[0].shape[1] // toks

    @pl.when(pl.program_id(0) == 0)
    def _():
        w_ref[...] = jnp.zeros_like(w_ref)

    group = 4
    eg = 8 if per % 8 == 0 else 1

    def one(k, carry):
        first = pl.multiple_of(k * group, group)
        right = g_ref[pl.ds(first, group)].reshape(group * toks, pair_ch)
        for h, o_ref in enumerate(o_refs):
            for e0 in range(0, per, eg):
                left = jnp.concatenate(
                    [
                        jnp.concatenate(
                            [
                                o_ref[
                                    pl.ds(pl.multiple_of((first + i) * chans, chans), chans),
                                    e * toks:(e + 1) * toks,
                                ]
                                for i in range(group)
                            ],
                            axis=1,
                        )
                        for e in range(e0, e0 + eg)
                    ],
                    axis=0,
                )
                at = (h * per + e0) * chans
                w_ref[at:at + eg * chans] += jnp.dot(left, right, preferred_element_type=F32)
        return carry

    lax.fori_loop(0, ti // group, one, 0)


def weight_call(outers, g, chans, ti):
    rows, toks, pair_ch = g.shape
    cols = outers[0].shape[1]
    width = cols * len(outers) // toks * chans
    return pl.pallas_call(
        functools.partial(weight_kernel, chans),
        out_shape=jax.ShapeDtypeStruct((width, pair_ch), F32),
        grid=(rows // ti,),
        in_specs=[pl.BlockSpec((ti * chans, cols), lambda m: (m, 0))] * len(outers)
        + [pl.BlockSpec((ti, toks, pair_ch), lambda m: (m, 0, 0))],
        out_specs=pl.BlockSpec((width, pair_ch), lambda m: (0, 0)),
        compiler_params=params(),
        cost_estimate=cost(4 * rows * toks * width * pair_ch, 2 * rows * toks * width),
        name="weight",
    )(*outers, g)


def fused_body(left_factor, right_factor, out_weight, pair_cotangent):
    seqs, chans, rows = left_factor.shape
    toks = right_factor.shape[2]
    pair_ch = out_weight.shape[1]
    inv = 1.0 / (seqs * lax.axis_size("depth"))
    n_col = lax.axis_size("col")
    parts = 4
    eb = chans // parts

    g = lax.all_gather(pair_cotangent, "depth", axis=0, tiled=True)
    a2 = jnp.transpose(left_factor, (0, 2, 1)).reshape(seqs, rows * chans)
    at = jnp.transpose(left_factor, (2, 1, 0)).reshape(rows * chans, seqs)
    b2 = right_factor.reshape(seqs, chans * toks)
    w_ec = jnp.transpose(out_weight.reshape(chans, chans, pair_ch), (1, 0, 2)).reshape(
        chans * chans, pair_ch
    )

    half_cols = b2.shape[1] // 2
    outer_a = outer_call(at, b2, inv, 16 * chans, eb * toks, 0, half_cols)
    g, outer_a = lax.optimization_barrier((g, outer_a))

    ds, rights = [], []
    for k in range(parts):
        d, r = delta_call(w_ec, g, a2, inv, chans, k, eb, 32)
        ds.append(d)
        r, g = lax.optimization_barrier((r, g))
        rights.append(lax.psum_scatter(r, "row", scatter_dimension=0, tiled=True))
    left = left_call(b2, ds, inv, 8 * chans)
    left, at, b2 = lax.optimization_barrier((left, at, b2))
    if n_col == 2:
        half = seqs // 2
        me = lax.axis_index("col")
        mine = lax.dynamic_slice_in_dim(left, me * half, half, 0)
        theirs = lax.dynamic_slice_in_dim(left, (1 - me) * half, half, 0)
        theirs, at, b2 = lax.optimization_barrier((theirs, at, b2))
        got = lax.ppermute(theirs, "col", [(0, 1), (1, 0)])
        left_grad = mine.astype(F32) + got.astype(F32)
    else:
        left_grad = lax.psum_scatter(left, "col", scatter_dimension=0, tiled=True).astype(F32)
    left_grad = jnp.transpose(left_grad.reshape(-1, rows, chans), (0, 2, 1))
    outer_b = outer_call(at, b2, inv, 16 * chans, eb * toks, 1, half_cols)
    weight_acc = weight_call((outer_a, outer_b), g, chans, 8)
    weight_acc = jnp.transpose(weight_acc.reshape(chans, chans, pair_ch), (1, 0, 2)).reshape(
        chans * chans, pair_ch
    )
    axes = ("depth", "row", "col")
    count = lax.axis_size(axes)
    pieces = weight_acc.reshape(count, chans * chans // count, pair_ch)
    pieces = lax.all_to_all(pieces, axes, split_axis=0, concat_axis=0, tiled=True)
    rights = [r.reshape(-1, eb, toks) for r in rights]
    right_grad = jnp.concatenate(rights, axis=1).astype(F32)
    pieces, left_grad, right_grad = lax.optimization_barrier((pieces, left_grad, right_grad))
    weight_grad = jnp.sum(pieces, axis=0)
    return left_grad, right_grad, weight_grad


def mega_kernel(
    dims, inv, a_hbm, bt_hbm, g_hbm, w_ref, eye_ref,
    rown, rfw, rfa, rfb, lown, lrecv, btr, wacc,
    a_all, d_all, b_all, g_all, stage, btc, fin, fsum,
    a_sem, g_loc, g_s, g_r, b_s, b_r, st_sem, fa_s, fa_r, fw_s, fw_r, fb_s, fb_r,
    l_s, l_r, btc_sem, fin_sem,
):
    chans, seqs, toks, nq, nl, quarter = dims
    n_depth, n_row, n_col = (lax.axis_size(x) for x in ("depth", "row", "col"))
    depth, row, col = (lax.axis_index(x) for x in ("depth", "row", "col"))
    core = lax.rem(depth, 2)
    buddy = depth + 1 - 2 * core
    pair = row + 1 - 2 * lax.rem(row, 2)
    far = 2 - 2 * (row // 2)
    inner = jnp.logical_or(row == 1, row == 2)
    jq = g_all.shape[0] // nq
    wide = jq * chans
    i_own = g_hbm.shape[2]
    lw = a_all.shape[1] // nl

    def remote(src, dst, ss, rs, **where):
        return pltpu.make_async_remote_copy(
            src_ref=src, dst_ref=dst, send_sem=ss, recv_sem=rs,
            device_id=where, device_id_type=MESH,
        )

    barrier = pltpu.get_barrier_semaphore()
    peers = [{"depth": lax.rem(depth + m, n_depth)} for m in range(1, n_depth)]
    peers += [{"row": lax.rem(row + m, n_row)} for m in range(1, n_row)]
    peers += [{"col": 1 - col}, {"depth": buddy, "col": 1 - col}]
    for where in peers:
        pl.semaphore_signal(barrier, inc=1, device_id=where, device_id_type=MESH)
    pl.semaphore_wait(barrier, len(peers))

    def g_copy(m, q):
        to = lax.rem(depth + m + 1, n_depth)
        js = pl.ds(pl.multiple_of(q * jq, jq), jq)
        rows = pl.ds(pl.multiple_of(depth * i_own, i_own), i_own)
        return remote(
            g_hbm.at[lax.rem(to, 2), js], g_all.at[js, rows], g_s.at[m, q], g_r.at[m, q], depth=to
        )

    def b_copy(q):
        rows = pl.ds(pl.multiple_of(q * wide, wide), wide)
        return remote(bt_hbm.at[1 - core, rows], btr.at[rows], b_s.at[q], b_r.at[q], depth=buddy)

    own_rows = pl.ds(pl.multiple_of(core * seqs, seqs), seqs)
    a_local = pltpu.make_async_copy(a_hbm, a_all.at[own_rows], a_sem.at[0])
    a_remote = remote(a_hbm, a_all.at[own_rows], a_sem.at[1], a_sem.at[2], depth=buddy)
    g_local = pltpu.make_async_copy(
        g_hbm.at[core], g_all.at[:, pl.ds(pl.multiple_of(depth * i_own, i_own), i_own)], g_loc.at[0]
    )
    for m in range(n_depth - 1):
        g_copy(m, 0).start()
    a_remote.start()
    g_local.start()
    a_local.start()

    def send_rest(q, carry):
        for m in range(n_depth - 1):
            g_copy(m, q).start()
        return carry

    lax.fori_loop(1, nq, send_rest, 0)

    def send_b(q, carry):
        b_copy(q).start()
        return carry

    lax.fori_loop(0, nq, send_b, 0)
    g_local.wait()
    a_local.wait()
    a_remote.wait()

    def bt_load(q, slot):
        rows = pl.ds(pl.multiple_of(q * wide, wide), wide)
        return (
            pltpu.make_async_copy(bt_hbm.at[core, rows], btc.at[slot, core], btc_sem.at[slot, 0]),
            pltpu.make_async_copy(btr.at[rows], btc.at[slot, 1 - core], btc_sem.at[slot, 1]),
        )

    def build_b(q):
        for cp in bt_load(q, 0):
            cp.wait()
        cols = pl.ds(pl.multiple_of(q * wide, wide), wide)
        for h in range(2):
            b_all[h * seqs:(h + 1) * seqs, cols] = lax.dot_general(
                eye_ref[...], btc[0, h], (((1,), (1,)), ((), ())), preferred_element_type=F32
            ).astype(BF16)

    def fa_copy(q):
        return remote(
            rown.at[q, pl.ds(2 * pair, 2)], rfa.at[q], fa_s.at[q], fa_r.at[q], row=pair
        )

    def fw_copy(q):
        return remote(
            rown.at[q, pl.ds(2 * far, 4)], rfw.at[q], fw_s.at[q], fw_r.at[q], row=pair
        )

    def fb_copy(m, u):
        return remote(
            fsum.at[lax.rem(m, 2), pl.ds(2 * u, 2)], rfb.at[m], fb_s.at[u, m], fb_r.at[m], row=far + u
        )

    def fin_loads(m):
        return (
            pltpu.make_async_copy(rfw.at[m], fin.at[0], fin_sem.at[0]),
            pltpu.make_async_copy(rown.at[m, pl.ds(2 * far, 4)], fin.at[1], fin_sem.at[1]),
        )

    def forward_start(m):
        fw_copy(m).wait_recv()
        for cp in fin_loads(m):
            cp.start()

    def forward_finish(m):
        for cp in fin_loads(m):
            cp.wait()

        @pl.when(m >= 2)
        def _():
            for u in range(2):
                fb_copy(m - 2, u).wait_send()

        fsum[lax.rem(m, 2)] = (fin[0].astype(F32) + fin[1].astype(F32)).astype(BF16)
        for u in range(2):
            fb_copy(m, u).start()

    def right_step(q, carry):
        turn = jnp.logical_and(inner, jnp.logical_and(q > 0, lax.rem(q, 3) == 0))
        m_now = jnp.maximum(q // 3 - 1, 0)

        @pl.when(turn)
        def _():
            forward_start(m_now)

        for m in range(n_depth - 1):
            g_copy(m, q).wait_recv()
        rows = pl.multiple_of(q * wide, wide)
        for u in range(jq // 2):
            pair_g = g_all[pl.ds(q * jq + 2 * u, 2)].reshape(2 * toks, -1)
            d = lax.dot_general(
                w_ref[...], pair_g, (((1,), (1,)), ((), ())), preferred_element_type=F32
            ).astype(BF16)
            for v in range(2):
                at = pl.multiple_of(rows + (2 * u + v) * chans, chans)
                for c in range(chans):
                    d_all[pl.ds(at, chans), c * toks:(c + 1) * toks] = d[
                        c * chans:(c + 1) * chans, v * toks:(v + 1) * toks
                    ]
        half = wide // 2
        for n in range(2):
            at = pl.multiple_of(rows + n * half, half)
            r = lax.dot_general(
                a_all[...], d_all[pl.ds(at, half)], (((1,), (1,)), ((), ())), preferred_element_type=F32
            )
            r = (r * inv).astype(BF16)
            for h in range(2):
                for t in range(n_row):
                    first = h * seqs + t * quarter
                    stage[0, 2 * t + h, :, n * half:(n + 1) * half] = r[first:first + quarter]
        out = pltpu.make_async_copy(stage.at[0], rown.at[q], st_sem.at[0])
        out.start()

        @pl.when(q > 0)
        def _():
            build_b(q - 1)

        b_copy(q).wait_recv()
        for cp in bt_load(q, 0):
            cp.start()
        out.wait()

        @pl.when(jnp.logical_not(inner))
        def _():
            fw_copy(q).start()

        fa_copy(q).start()

        @pl.when(turn)
        def _():
            forward_finish(m_now)

        return carry

    lax.fori_loop(0, nq, right_step, 0)
    build_b(nq - 1)

    def l_copy(l, r):
        kk = core if r == 1 else 1 - core
        tx = col if r == 0 else 1 - col
        where = ({"depth": buddy}, {"col": 1 - col}, {"depth": buddy, "col": 1 - col})[r]
        return remote(
            lown.at[l, pl.ds((kk * 2 + tx) * 2, 2)], lrecv.at[r, l], l_s.at[r, l], l_r.at[r, l], **where
        )

    def l_out(l):
        slot = lax.rem(l, 2)
        return pltpu.make_async_copy(stage.at[slot], lown.at[l], st_sem.at[slot])

    def l_send(l):
        l_out(l).wait()
        for r in (2, 1, 0):
            l_copy(l, r).start()

    def left_step(l, carry):
        turn = jnp.logical_and(inner, lax.rem(l, 4) == 0)
        m_now = 2 + l // 4

        @pl.when(turn)
        def _():
            forward_start(m_now)

        half = lw // 2
        slot = lax.rem(l, 2)
        for n in range(2):
            cols = pl.ds(pl.multiple_of(l * lw + n * half, half), half)
            x = jnp.dot(b_all[...], d_all[:, cols], preferred_element_type=F32)
            x = (x * inv).astype(BF16)
            for t in range(2 * n_row):
                stage[slot, t, :, n * half:(n + 1) * half] = x[t * quarter:(t + 1) * quarter]
        l_out(l).start()

        @pl.when(l > 0)
        def _():
            l_send(l - 1)

        @pl.when(turn)
        def _():
            forward_finish(m_now)

        return carry

    for cp in bt_load(0, 0):
        cp.start()
    lax.fori_loop(0, nl, left_step, 0)
    l_send(nl - 1)

    wacc[...] = jnp.zeros_like(wacc)

    def outer_step(o, carry):
        turn = jnp.logical_and(inner, lax.rem(o, 3) == 0)
        m_now = 4 + o // 3

        @pl.when(turn)
        def _():
            forward_start(m_now)

        slot = lax.rem(o, 2)
        for cp in bt_load(o, slot):
            cp.wait()

        @pl.when(o < nq - 1)
        def _():
            for cp in bt_load(o + 1, 1 - slot):
                cp.start()

        width = 512
        for n in range(a_all.shape[1] // width):
            cols = slice(n * width, (n + 1) * width)
            x = jnp.dot(btc[slot, 0], a_all[:seqs, cols], preferred_element_type=F32)
            x += jnp.dot(btc[slot, 1], a_all[seqs:, cols], preferred_element_type=F32)
            d_all[:wide, cols] = (x * inv).astype(BF16)
        right = g_all[pl.ds(pl.multiple_of(o * jq, jq), jq)].reshape(jq * toks, -1)
        cg = 8
        for c0 in range(0, chans, cg):
            left = jnp.concatenate(
                [
                    jnp.concatenate(
                        [
                            d_all[j * chans:(j + 1) * chans, c * toks:(c + 1) * toks]
                            for j in range(jq)
                        ],
                        axis=1,
                    )
                    for c in range(c0, c0 + cg)
                ],
                axis=0,
            )
            wacc[c0 * chans:(c0 + cg) * chans] += jnp.dot(left, right, preferred_element_type=F32)

        @pl.when(turn)
        def _():
            forward_finish(m_now)

        return carry

    lax.fori_loop(0, nq, outer_step, 0)

    @pl.when(inner)
    def _():
        forward_start(nq - 1)
        forward_finish(nq - 1)
        for m in (nq - 2, nq - 1):
            for u in range(2):
                fb_copy(m, u).wait_send()

    def drain(q, carry):
        for m in range(n_depth - 1):
            g_copy(m, q).wait_send()
        b_copy(q).wait_send()
        fa_copy(q).wait()

        @pl.when(jnp.logical_not(inner))
        def _():
            fw_copy(q).wait_send()

        fb_copy(q, 0).wait_recv()
        return carry

    lax.fori_loop(0, nq, drain, 0)

    def drain_l(l, carry):
        for r in range(3):
            l_copy(l, r).wait()
        return carry

    lax.fori_loop(0, nl, drain_l, 0)


def mega_call(a2, bt, gt, w, inv, chans, toks):
    seqs, ci = a2.shape
    jh, je = gt.shape[1], bt.shape[1]
    i_own, pair_ch = gt.shape[2:]
    n_depth, n_row = lax.axis_size("depth"), lax.axis_size("row")
    nq = nl = 8
    wide = je // nq
    lw = ci // nl
    quarter = seqs // n_row
    hbm = lambda *s: jax.ShapeDtypeStruct(s, BF16)
    dma = lambda *s: pltpu.SemaphoreType.DMA(s)
    anyspec = pl.BlockSpec(memory_space=pl.ANY)
    vmem = pl.BlockSpec(memory_space=pltpu.VMEM)
    eye = jnp.eye(seqs, dtype=BF16)
    return pl.pallas_call(
        functools.partial(mega_kernel, (chans, seqs, toks, nq, nl, quarter), inv),
        out_shape=(
            hbm(nq, 2 * n_row, quarter, wide),
            hbm(nq, 4, quarter, wide),
            hbm(nq, 2, quarter, wide),
            hbm(nq, 2, quarter, wide),
            hbm(nl, 2 * n_row, quarter, lw),
            hbm(3, nl, 2, quarter, lw),
            hbm(je, seqs),
            jax.ShapeDtypeStruct((chans * chans, pair_ch), F32),
        ),
        in_specs=[anyspec, anyspec, anyspec, vmem, vmem],
        out_specs=(anyspec,) * 7 + (vmem,),
        scratch_shapes=[
            pltpu.VMEM((2 * seqs, ci), BF16),
            pltpu.VMEM((je, ci), BF16),
            pltpu.VMEM((2 * seqs, je), BF16),
            pltpu.VMEM((jh, i_own * n_depth, pair_ch), BF16),
            pltpu.VMEM((2, 2 * n_row, quarter, wide), BF16),
            pltpu.VMEM((2, 2, wide, seqs), BF16),
            pltpu.VMEM((2, 4, quarter, wide), BF16),
            pltpu.VMEM((2, 4, quarter, wide), BF16),
            dma(3), dma(1), dma(n_depth - 1, nq), dma(n_depth - 1, nq), dma(nq), dma(nq), dma(2),
            dma(nq), dma(nq), dma(nq), dma(nq), dma(2, nq), dma(nq),
            dma(3, nl), dma(3, nl), dma(2, 2), dma(2),
        ],
        compiler_params=pltpu.CompilerParams(
            vmem_limit_bytes=MEGA_VMEM, collective_id=0, has_side_effects=True
        ),
        cost_estimate=cost(6 * seqs * 2 * je * ci, 8 * seqs * ci),
        name="mega",
    )(a2, bt, gt, w, eye)


def mega_body(left_factor, right_factor, out_weight, pair_cotangent):
    seqs, chans, rows = left_factor.shape
    toks = right_factor.shape[2]
    pair_ch = out_weight.shape[1]
    inv = 1.0 / (seqs * lax.axis_size("depth"))
    jh = toks // 2
    n_depth, n_row = lax.axis_size("depth"), lax.axis_size("row")
    quarter = seqs // n_row
    depth, row, col = (lax.axis_index(x) for x in ("depth", "row", "col"))
    core = lax.rem(depth, 2)

    a2 = left_factor.reshape(seqs, chans * rows)
    bt = jnp.transpose(right_factor, (2, 1, 0)).reshape(2, jh * chans, seqs)
    gt = jnp.transpose(pair_cotangent, (1, 0, 2)).reshape(2, jh, -1, pair_ch)
    rown, _, rfa, rfb, lown, lrecv, _, wacc = mega_call(a2, bt, gt, out_weight, inv, chans, rows)

    axes = ("depth", "row", "col")
    count = lax.axis_size(axes)
    pieces = wacc.reshape(count, chans * chans // count, pair_ch)
    pieces = lax.all_to_all(pieces, axes, split_axis=0, concat_axis=0, tiled=True)

    total = lax.dynamic_slice_in_dim(rown, 2 * row, 2, 1).astype(F32)
    total = (total + rfa.astype(F32) + rfb.astype(F32)).astype(BF16)
    mine = lax.dynamic_slice_in_dim(total, core, 1, 1)
    theirs = lax.dynamic_slice_in_dim(total, 1 - core, 1, 1)
    swap = [(d, d + 1 - 2 * (d % 2)) for d in range(n_depth)]
    got = lax.ppermute(theirs, "depth", swap)
    low = jnp.where(core == 0, mine, got)
    high = jnp.where(core == 0, got, mine)
    both = jnp.concatenate([low, high], axis=1)
    nq = both.shape[0]
    both = both.reshape(nq, 2, quarter, jh // nq, chans)
    right_grad = jnp.transpose(both, (2, 4, 1, 0, 3)).reshape(quarter, chans, toks).astype(F32)

    first = (core * 2 + col) * 2
    left = lax.dynamic_slice_in_dim(lown, first, 2, 1).astype(F32)
    for r in range(lrecv.shape[0]):
        left = left + lrecv[r].astype(F32)
    nl = left.shape[0]
    left = left.reshape(nl, 2 * quarter, chans // nl, rows)
    left_grad = jnp.transpose(left, (1, 0, 2, 3)).reshape(2 * quarter, chans, rows)
    return left_grad, right_grad, jnp.sum(pieces, axis=0)


def plain_body(left_factor, right_factor, out_weight, pair_cotangent):
    seq_total = left_factor.shape[0] * lax.axis_size("depth")
    chans = left_factor.shape[1]
    rows_here = left_factor.shape[2]
    cols_here = right_factor.shape[2]
    width = out_weight.shape[0]
    pair_ch = out_weight.shape[1]
    natural = jnp.einsum("sci,sej->ciej", left_factor, right_factor, preferred_element_type=F32) / seq_total
    outer = jnp.transpose(natural.astype(BF16), (1, 3, 0, 2)).reshape(rows_here * cols_here, width)
    piece = lax.all_gather(pair_cotangent, "depth", axis=0, tiled=True)
    grad_two = piece.reshape(rows_here * cols_here, pair_ch)
    delta = jnp.dot(grad_two, out_weight.T, preferred_element_type=F32).astype(BF16)
    weight_acc = jnp.dot(outer.T, grad_two, preferred_element_type=F32)
    delta_four = delta.reshape(rows_here, cols_here, chans, chans)
    left_part = jnp.einsum("ijce,sej->sci", delta_four, right_factor, preferred_element_type=F32) / seq_total
    right_part = jnp.einsum("ijce,sci->sej", delta_four, left_factor, preferred_element_type=F32) / seq_total
    left_grad = lax.psum_scatter(left_part, "col", scatter_dimension=0, tiled=True)
    right_grad = lax.psum_scatter(right_part, "row", scatter_dimension=0, tiled=True)
    middle = lax.psum_scatter(weight_acc, ("depth", "row"), scatter_dimension=0, tiled=True)
    weight_grad = lax.psum_scatter(middle, "col", scatter_dimension=0, tiled=True)
    return left_grad, right_grad, weight_grad


def body(left_factor, right_factor, out_weight, pair_cotangent):
    seqs, chans, rows = left_factor.shape
    toks = right_factor.shape[2]
    fits = toks % 128 == 0 and toks <= 256 and rows % 32 == 0 and chans == 32 and seqs <= 512
    shape = tuple(lax.axis_size(x) for x in ("depth", "row", "col"))
    mega = (
        fits and shape == (4, 4, 2) and toks == 256 and rows == 128 and seqs % 64 == 0
        and out_weight.shape[1] == 128
    )
    run = mega_body if mega else fused_body if fits else plain_body
    return run(left_factor, right_factor, out_weight, pair_cotangent)


def solution(mesh):
    return jax.shard_map(
        body,
        mesh=mesh,
        in_specs=(
            P("depth", None, "row"),
            P("depth", None, "col"),
            P(),
            P(("row", "depth"), "col", None),
        ),
        out_specs=(
            P(("depth", "col"), None, "row"),
            P(("depth", "row"), None, "col"),
            P(("depth", "row", "col"), None),
        ),
        check_vma=False,
    )
```

```python
import functools

import jax
import jax.numpy as jnp
from jax import lax
from jax.experimental import pallas as pl
from jax.experimental.pallas import tpu as pltpu
from jax.sharding import PartitionSpec as P

F32 = jnp.float32
BF16 = jnp.bfloat16
VMEM_CAP = 60 * 1024 * 1024
MEGA_VMEM = 62 * 1024 * 1024
MESH = pl.DeviceIdType.MESH


def params():
    return pltpu.CompilerParams(vmem_limit_bytes=VMEM_CAP)


def cost(flops, nbytes):
    return pl.CostEstimate(flops=flops, bytes_accessed=nbytes, transcendentals=0)


def outer_kernel(inv, at_ref, b_ref, o_ref):
    width = 512 if o_ref.shape[1] % 512 == 0 else o_ref.shape[1]
    for n in range(o_ref.shape[1] // width):
        cols = slice(n * width, (n + 1) * width)
        acc = jnp.dot(at_ref[...], b_ref[:, cols], preferred_element_type=F32)
        o_ref[:, cols] = (acc * inv).astype(BF16)


def outer_call(at, b2, inv, tm, tn, part, cols):
    rows, seqs = at.shape
    first = part * cols // tn
    return pl.pallas_call(
        functools.partial(outer_kernel, inv),
        out_shape=jax.ShapeDtypeStruct((rows, cols), BF16),
        grid=(cols // tn, rows // tm),
        in_specs=[
            pl.BlockSpec((tm, seqs), lambda n, m: (m, 0)),
            pl.BlockSpec((seqs, tn), lambda n, m: (0, n + first)),
        ],
        out_specs=pl.BlockSpec((tm, tn), lambda n, m: (m, n)),
        compiler_params=params(),
        cost_estimate=cost(2 * rows * cols * seqs, 2 * rows * cols + 2 * seqs * (rows + cols)),
        name=f"outer_{part}",
    )(at, b2)


def delta_kernel(inv, chans, toks, w_ref, g_ref, a_ref, d_ref, r_ref, acc_ref):
    step = pl.program_id(0)
    here = g_ref.shape[0]
    eb = w_ref.shape[0] // chans

    def one(i, carry):
        d = lax.dot_general(
            w_ref[...], g_ref[i], (((1,), (1,)), ((), ())), preferred_element_type=F32
        ).astype(BF16)
        at = pl.multiple_of(i * chans, chans)
        for e in range(eb):
            d_ref[pl.ds(at, chans), e * toks:(e + 1) * toks] = d[e * chans:(e + 1) * chans]
        return carry

    lax.fori_loop(0, here, one, 0, unroll=8)

    @pl.when(step == 0)
    def _():
        acc_ref[...] = jnp.zeros_like(acc_ref)

    for e in range(eb):
        cols = slice(e * toks, (e + 1) * toks)
        acc_ref[:, cols] += jnp.dot(a_ref[...], d_ref[:, cols], preferred_element_type=F32)

    @pl.when(step == pl.num_programs(0) - 1)
    def _():
        r_ref[...] = (acc_ref[...] * inv).astype(BF16)


def delta_call(w_ec, g, a2, inv, chans, part, eb, ti):
    rows, toks, pair_ch = g.shape
    seqs = a2.shape[0]
    wide = eb * toks
    return pl.pallas_call(
        functools.partial(delta_kernel, inv, chans, toks),
        out_shape=(
            jax.ShapeDtypeStruct((rows * chans, wide), BF16),
            jax.ShapeDtypeStruct((seqs, wide), BF16),
        ),
        grid=(rows // ti,),
        in_specs=[
            pl.BlockSpec((eb * chans, pair_ch), lambda m: (part, 0)),
            pl.BlockSpec((ti, toks, pair_ch), lambda m: (m, 0, 0)),
            pl.BlockSpec((seqs, ti * chans), lambda m: (0, m)),
        ],
        out_specs=(
            pl.BlockSpec((ti * chans, wide), lambda m: (m, 0)),
            pl.BlockSpec((seqs, wide), lambda m: (0, 0)),
        ),
        scratch_shapes=[pltpu.VMEM((seqs, wide), F32)],
        compiler_params=params(),
        cost_estimate=cost(
            2 * rows * chans * wide * (seqs + 2 * pair_ch),
            2 * rows * (chans * wide + toks * pair_ch + chans * seqs),
        ),
        name=f"delta_right_{part}",
    )(w_ec, g, a2)


def left_kernel(inv, parts, b_ref, *refs):
    d_refs, o_ref = refs[:parts], refs[parts]
    wide = d_refs[0].shape[1]
    acc = None
    for k in range(parts):
        term = lax.dot_general(
            b_ref[:, k * wide:(k + 1) * wide],
            d_refs[k][...],
            (((1,), (1,)), ((), ())),
            preferred_element_type=F32,
        )
        acc = term if acc is None else acc + term
    o_ref[...] = (acc * inv).astype(BF16)


def left_call(b2, ds, inv, tn):
    seqs = b2.shape[0]
    rows, wide = ds[0].shape
    parts = len(ds)
    return pl.pallas_call(
        functools.partial(left_kernel, inv, parts),
        out_shape=jax.ShapeDtypeStruct((seqs, rows), BF16),
        grid=(rows // tn,),
        in_specs=[pl.BlockSpec((seqs, parts * wide), lambda m: (0, 0))]
        + [pl.BlockSpec((tn, wide), lambda m: (m, 0))] * parts,
        out_specs=pl.BlockSpec((seqs, tn), lambda m: (0, m)),
        compiler_params=params(),
        cost_estimate=cost(2 * seqs * rows * wide * parts, 2 * rows * wide * parts + 4 * seqs * rows),
        name="left",
    )(b2, *ds)


def weight_kernel(chans, *refs):
    o_refs, g_ref, w_ref = refs[:-2], refs[-2], refs[-1]
    ti, toks, pair_ch = g_ref.shape
    per = o_refs[0].shape[1] // toks

    @pl.when(pl.program_id(0) == 0)
    def _():
        w_ref[...] = jnp.zeros_like(w_ref)

    group = 4
    eg = 8 if per % 8 == 0 else 1

    def one(k, carry):
        first = pl.multiple_of(k * group, group)
        right = g_ref[pl.ds(first, group)].reshape(group * toks, pair_ch)
        for h, o_ref in enumerate(o_refs):
            for e0 in range(0, per, eg):
                left = jnp.concatenate(
                    [
                        jnp.concatenate(
                            [
                                o_ref[
                                    pl.ds(pl.multiple_of((first + i) * chans, chans), chans),
                                    e * toks:(e + 1) * toks,
                                ]
                                for i in range(group)
                            ],
                            axis=1,
                        )
                        for e in range(e0, e0 + eg)
                    ],
                    axis=0,
                )
                at = (h * per + e0) * chans
                w_ref[at:at + eg * chans] += jnp.dot(left, right, preferred_element_type=F32)
        return carry

    lax.fori_loop(0, ti // group, one, 0)


def weight_call(outers, g, chans, ti):
    rows, toks, pair_ch = g.shape
    cols = outers[0].shape[1]
    width = cols * len(outers) // toks * chans
    return pl.pallas_call(
        functools.partial(weight_kernel, chans),
        out_shape=jax.ShapeDtypeStruct((width, pair_ch), F32),
        grid=(rows // ti,),
        in_specs=[pl.BlockSpec((ti * chans, cols), lambda m: (m, 0))] * len(outers)
        + [pl.BlockSpec((ti, toks, pair_ch), lambda m: (m, 0, 0))],
        out_specs=pl.BlockSpec((width, pair_ch), lambda m: (0, 0)),
        compiler_params=params(),
        cost_estimate=cost(4 * rows * toks * width * pair_ch, 2 * rows * toks * width),
        name="weight",
    )(*outers, g)


def fused_body(left_factor, right_factor, out_weight, pair_cotangent):
    seqs, chans, rows = left_factor.shape
    toks = right_factor.shape[2]
    pair_ch = out_weight.shape[1]
    inv = 1.0 / (seqs * lax.axis_size("depth"))
    n_col = lax.axis_size("col")
    parts = 4
    eb = chans // parts

    g = lax.all_gather(pair_cotangent, "depth", axis=0, tiled=True)
    a2 = jnp.transpose(left_factor, (0, 2, 1)).reshape(seqs, rows * chans)
    at = jnp.transpose(left_factor, (2, 1, 0)).reshape(rows * chans, seqs)
    b2 = right_factor.reshape(seqs, chans * toks)
    w_ec = jnp.transpose(out_weight.reshape(chans, chans, pair_ch), (1, 0, 2)).reshape(
        chans * chans, pair_ch
    )

    half_cols = b2.shape[1] // 2
    outer_a = outer_call(at, b2, inv, 16 * chans, eb * toks, 0, half_cols)
    g, outer_a = lax.optimization_barrier((g, outer_a))

    ds, rights = [], []
    for k in range(parts):
        d, r = delta_call(w_ec, g, a2, inv, chans, k, eb, 32)
        ds.append(d)
        r, g = lax.optimization_barrier((r, g))
        rights.append(lax.psum_scatter(r, "row", scatter_dimension=0, tiled=True))
    left = left_call(b2, ds, inv, 8 * chans)
    left, at, b2 = lax.optimization_barrier((left, at, b2))
    if n_col == 2:
        half = seqs // 2
        me = lax.axis_index("col")
        mine = lax.dynamic_slice_in_dim(left, me * half, half, 0)
        theirs = lax.dynamic_slice_in_dim(left, (1 - me) * half, half, 0)
        theirs, at, b2 = lax.optimization_barrier((theirs, at, b2))
        got = lax.ppermute(theirs, "col", [(0, 1), (1, 0)])
        left_grad = mine.astype(F32) + got.astype(F32)
    else:
        left_grad = lax.psum_scatter(left, "col", scatter_dimension=0, tiled=True).astype(F32)
    left_grad = jnp.transpose(left_grad.reshape(-1, rows, chans), (0, 2, 1))
    outer_b = outer_call(at, b2, inv, 16 * chans, eb * toks, 1, half_cols)
    weight_acc = weight_call((outer_a, outer_b), g, chans, 8)
    weight_acc = jnp.transpose(weight_acc.reshape(chans, chans, pair_ch), (1, 0, 2)).reshape(
        chans * chans, pair_ch
    )
    axes = ("depth", "row", "col")
    count = lax.axis_size(axes)
    pieces = weight_acc.reshape(count, chans * chans // count, pair_ch)
    pieces = lax.all_to_all(pieces, axes, split_axis=0, concat_axis=0, tiled=True)
    rights = [r.reshape(-1, eb, toks) for r in rights]
    right_grad = jnp.concatenate(rights, axis=1).astype(F32)
    pieces, left_grad, right_grad = lax.optimization_barrier((pieces, left_grad, right_grad))
    weight_grad = jnp.sum(pieces, axis=0)
    return left_grad, right_grad, weight_grad


def mega_kernel(
    dims, inv, a_hbm, bt_hbm, g_hbm, w_ref, eye_ref,
    rown, rfw, rfa, rfb, lown, lrecv, btr, rfin, left_out, wacc,
    a_all, d_all, b_all, g_all, stage, btc, fin, fsum, lbuf,
    a_sem, g_loc, g_s, g_r, b_s, b_r, st_sem, fa_s, fa_r, fw_s, fw_r, fb_s, fb_r,
    l_s, l_r, btc_sem, fin_sem, rx_s, rx_r, rx_l, rl_sem, ll_sem, lo_sem,
):
    chans, seqs, toks, nq, nl, quarter = dims
    n_depth, n_row, n_col = (lax.axis_size(x) for x in ("depth", "row", "col"))
    depth, row, col = (lax.axis_index(x) for x in ("depth", "row", "col"))
    core = lax.rem(depth, 2)
    buddy = depth + 1 - 2 * core
    pair = row + 1 - 2 * lax.rem(row, 2)
    far = 2 - 2 * (row // 2)
    inner = jnp.logical_or(row == 1, row == 2)
    jq = g_all.shape[0] // nq
    wide = jq * chans
    i_own = g_hbm.shape[2]
    lw = a_all.shape[1] // nl

    def remote(src, dst, ss, rs, **where):
        return pltpu.make_async_remote_copy(
            src_ref=src, dst_ref=dst, send_sem=ss, recv_sem=rs,
            device_id=where, device_id_type=MESH,
        )

    barrier = pltpu.get_barrier_semaphore()
    peers = [{"depth": lax.rem(depth + m, n_depth)} for m in range(1, n_depth)]
    peers += [{"row": lax.rem(row + m, n_row)} for m in range(1, n_row)]
    peers += [{"col": 1 - col}, {"depth": buddy, "col": 1 - col}]
    for where in peers:
        pl.semaphore_signal(barrier, inc=1, device_id=where, device_id_type=MESH)
    pl.semaphore_wait(barrier, len(peers))

    def g_copy(m, q):
        to = lax.rem(depth + m + 1, n_depth)
        js = pl.ds(pl.multiple_of(q * jq, jq), jq)
        rows = pl.ds(pl.multiple_of(depth * i_own, i_own), i_own)
        return remote(
            g_hbm.at[lax.rem(to, 2), js], g_all.at[js, rows], g_s.at[m, q], g_r.at[m, q], depth=to
        )

    def b_copy(q):
        rows = pl.ds(pl.multiple_of(q * wide, wide), wide)
        return remote(bt_hbm.at[1 - core, rows], btr.at[rows], b_s.at[q], b_r.at[q], depth=buddy)

    own_rows = pl.ds(pl.multiple_of(core * seqs, seqs), seqs)
    a_local = pltpu.make_async_copy(a_hbm, a_all.at[own_rows], a_sem.at[0])
    a_remote = remote(a_hbm, a_all.at[own_rows], a_sem.at[1], a_sem.at[2], depth=buddy)
    g_local = pltpu.make_async_copy(
        g_hbm.at[core], g_all.at[:, pl.ds(pl.multiple_of(depth * i_own, i_own), i_own)], g_loc.at[0]
    )
    for m in range(n_depth - 1):
        g_copy(m, 0).start()
    a_remote.start()
    g_local.start()
    a_local.start()

    def send_rest(q, carry):
        for m in range(n_depth - 1):
            g_copy(m, q).start()
        return carry

    lax.fori_loop(1, nq, send_rest, 0)

    def send_b(q, carry):
        b_copy(q).start()
        return carry

    lax.fori_loop(0, nq, send_b, 0)
    g_local.wait()
    a_local.wait()
    a_remote.wait()

    def bt_load(q, slot):
        rows = pl.ds(pl.multiple_of(q * wide, wide), wide)
        return (
            pltpu.make_async_copy(bt_hbm.at[core, rows], btc.at[slot, core], btc_sem.at[slot, 0]),
            pltpu.make_async_copy(btr.at[rows], btc.at[slot, 1 - core], btc_sem.at[slot, 1]),
        )

    def build_b(q):
        for cp in bt_load(q, 0):
            cp.wait()
        cols = pl.ds(pl.multiple_of(q * wide, wide), wide)
        for h in range(2):
            b_all[h * seqs:(h + 1) * seqs, cols] = lax.dot_general(
                eye_ref[...], btc[0, h], (((1,), (1,)), ((), ())), preferred_element_type=F32
            ).astype(BF16)

    piece = 2 * quarter

    def target(t, count):
        return pl.ds(pl.multiple_of(t * piece, piece), count * piece)

    def fa_copy(q):
        return remote(
            rown.at[q, target(pair, 1)], rfa.at[q], fa_s.at[q], fa_r.at[q], row=pair
        )

    def fw_copy(q):
        return remote(
            rown.at[q, target(far, 2)], rfw.at[q], fw_s.at[q], fw_r.at[q], row=pair
        )

    def fb_copy(m, u):
        return remote(
            fsum.at[lax.rem(m, 2), u * piece:(u + 1) * piece], rfb.at[m], fb_s.at[u, m], fb_r.at[m], row=far + u
        )

    def fin_loads(m):
        return (
            pltpu.make_async_copy(rfw.at[m], fin.at[0], fin_sem.at[0]),
            pltpu.make_async_copy(rown.at[m, target(far, 2)], fin.at[1], fin_sem.at[1]),
        )

    def forward_start(m):
        fw_copy(m).wait_recv()
        for cp in fin_loads(m):
            cp.start()

    def forward_finish(m):
        for cp in fin_loads(m):
            cp.wait()

        @pl.when(m >= 2)
        def _():
            for u in range(2):
                fb_copy(m - 2, u).wait_send()

        fsum[lax.rem(m, 2)] = (fin[0].astype(F32) + fin[1].astype(F32)).astype(BF16)
        for u in range(2):
            fb_copy(m, u).start()

    def right_step(q, carry):
        turn = jnp.logical_and(inner, jnp.logical_and(q > 0, lax.rem(q, 3) == 0))
        m_now = jnp.maximum(q // 3 - 1, 0)

        @pl.when(turn)
        def _():
            forward_start(m_now)

        for m in range(n_depth - 1):
            g_copy(m, q).wait_recv()
        rows = pl.multiple_of(q * wide, wide)
        for u in range(jq // 2):
            pair_g = g_all[pl.ds(q * jq + 2 * u, 2)].reshape(2 * toks, -1)
            d = lax.dot_general(
                w_ref[...], pair_g, (((1,), (1,)), ((), ())), preferred_element_type=F32
            ).astype(BF16)
            for v in range(2):
                at = pl.multiple_of(rows + (2 * u + v) * chans, chans)
                for c in range(chans):
                    d_all[pl.ds(at, chans), c * toks:(c + 1) * toks] = d[
                        c * chans:(c + 1) * chans, v * toks:(v + 1) * toks
                    ]
        half = wide // 2
        for n in range(2):
            at = pl.multiple_of(rows + n * half, half)
            r = lax.dot_general(
                a_all[...], d_all[pl.ds(at, half)], (((1,), (1,)), ((), ())), preferred_element_type=F32
            )
            r = (r * inv).astype(BF16)
            for h in range(2):
                for t in range(n_row):
                    first = h * seqs + t * quarter
                    at = t * piece + h * quarter
                    stage[0, at:at + quarter, n * half:(n + 1) * half] = r[first:first + quarter]
        out = pltpu.make_async_copy(stage.at[0], rown.at[q], st_sem.at[0])
        out.start()

        @pl.when(q > 0)
        def _():
            build_b(q - 1)

        b_copy(q).wait_recv()
        for cp in bt_load(q, 0):
            cp.start()
        out.wait()

        @pl.when(jnp.logical_not(inner))
        def _():
            fw_copy(q).start()

        fa_copy(q).start()

        @pl.when(turn)
        def _():
            forward_finish(m_now)

        return carry

    lax.fori_loop(0, nq, right_step, 0)
    build_b(nq - 1)

    def l_copy(l, r):
        kk = core if r == 1 else 1 - core
        tx = col if r == 0 else 1 - col
        where = ({"depth": buddy}, {"col": 1 - col}, {"depth": buddy, "col": 1 - col})[r]
        return remote(
            lown.at[l, target(kk * 2 + tx, 1)], lrecv.at[r, l], l_s.at[r, l], l_r.at[r, l], **where
        )

    def l_out(l):
        slot = lax.rem(l, 2)
        return pltpu.make_async_copy(stage.at[slot], lown.at[l], st_sem.at[slot])

    def l_send(l):
        l_out(l).wait()
        for r in (2, 1, 0):
            l_copy(l, r).start()

    def left_step(l, carry):
        turn = jnp.logical_and(inner, lax.rem(l, 4) == 0)
        m_now = 2 + l // 4

        @pl.when(turn)
        def _():
            forward_start(m_now)

        half = lw // 2
        slot = lax.rem(l, 2)
        for n in range(2):
            cols = pl.ds(pl.multiple_of(l * lw + n * half, half), half)
            x = jnp.dot(b_all[...], d_all[:, cols], preferred_element_type=F32)
            x = (x * inv).astype(BF16)
            stage[slot, :, n * half:(n + 1) * half] = x
        l_out(l).start()

        @pl.when(l > 0)
        def _():
            l_send(l - 1)

        @pl.when(turn)
        def _():
            forward_finish(m_now)

        return carry

    for cp in bt_load(0, 0):
        cp.start()
    lax.fori_loop(0, nl, left_step, 0)
    l_send(nl - 1)

    wacc[...] = jnp.zeros_like(wacc)

    def right_loads(m):
        srcs = (rown.at[m, target(row, 1)], rfa.at[m], rfb.at[m])
        return [
            pltpu.make_async_copy(
                src, b_all.at[n * piece:(n + 1) * piece, 7 * wide:8 * wide], rl_sem.at[n]
            )
            for n, src in enumerate(srcs)
        ]

    def right_out(m):
        slot = lax.rem(m, 2)
        cols = pl.ds(pl.multiple_of((core * nq + m) * wide, wide), wide)

        def rows(k):
            at = slot * piece + k * quarter
            return b_all.at[pl.ds(pl.multiple_of(at, quarter), quarter), 6 * wide:7 * wide]

        return (
            pltpu.make_async_copy(rows(core), rfin.at[:, cols], rx_l.at[m]),
            remote(rows(1 - core), rfin.at[:, cols], rx_s.at[m], rx_r.at[m], depth=buddy),
        )

    def right_final_start(m):
        fa_copy(m).wait_recv()
        fb_copy(m, 0).wait_recv()
        for cp in right_loads(m):
            cp.start()

    def right_final_finish(m):
        for cp in right_loads(m):
            cp.wait()

        @pl.when(m >= 2)
        def _():
            mine, theirs = right_out(m - 2)
            mine.wait()
            theirs.wait_send()

        total = sum(
            b_all[n * piece:(n + 1) * piece, 7 * wide:8 * wide].astype(F32) for n in range(3)
        ).astype(BF16)
        at = pl.multiple_of(lax.rem(m, 2) * piece, piece)
        b_all[pl.ds(at, piece), 6 * wide:7 * wide] = total
        for cp in right_out(m):
            cp.start()

    def left_loads(p):
        cps = []
        for h in range(2):
            l = 2 * p + h
            srcs = [lown.at[l, target(core * 2 + col, 1)]] + [lrecv.at[r, l] for r in range(3)]
            for n, src in enumerate(srcs):
                dst = b_all.at[n * piece:(n + 1) * piece, h * lw:(h + 1) * lw]
                cps.append(pltpu.make_async_copy(src, dst, ll_sem.at[h, n]))
        return cps

    def left_out_copy(p):
        cs = pl.ds(pl.multiple_of(p * 8, 8), 8)
        return pltpu.make_async_copy(lbuf.reshape(piece, 8, toks), left_out.at[:, cs], lo_sem.at[0])

    def left_final_start(p):
        for h in range(2):
            for r in range(3):
                l_copy(2 * p + h, r).wait_recv()
        for cp in left_loads(p):
            cp.start()

    def left_final_finish(p):
        for cp in left_loads(p):
            cp.wait()

        @pl.when(p >= 1)
        def _():
            left_out_copy(p - 1).wait()

        for h in range(2):
            for c in range(4):
                cols = slice(h * lw + c * toks, h * lw + (c + 1) * toks)
                lbuf[pl.ds(4 * h + c, piece, stride=8), :] = sum(
                    b_all[n * piece:(n + 1) * piece, cols].astype(F32) for n in range(4)
                )
        left_out_copy(p).start()

    def outer_step(o, carry):
        turn = jnp.logical_and(inner, lax.rem(o, 3) == 0)
        m_now = 4 + o // 3
        left_turn = jnp.logical_or(o == 1, jnp.logical_or(o == 3, o == 6))
        p_now = o // 3

        @pl.when(turn)
        def _():
            forward_start(m_now)

        @pl.when(o < early)
        def _():
            right_final_start(o)

        @pl.when(left_turn)
        def _():
            left_final_start(p_now)

        slot = lax.rem(o, 2)
        for cp in bt_load(o, slot):
            cp.wait()

        @pl.when(o < nq - 1)
        def _():
            for cp in bt_load(o + 1, 1 - slot):
                cp.start()

        width = 512
        for n in range(a_all.shape[1] // width):
            cols = slice(n * width, (n + 1) * width)
            x = jnp.dot(btc[slot, 0], a_all[:seqs, cols], preferred_element_type=F32)
            x += jnp.dot(btc[slot, 1], a_all[seqs:, cols], preferred_element_type=F32)
            d_all[:wide, cols] = (x * inv).astype(BF16)
        right = g_all[pl.ds(pl.multiple_of(o * jq, jq), jq)].reshape(jq * toks, -1)
        cg = 8
        for c0 in range(0, chans, cg):
            left = jnp.concatenate(
                [
                    jnp.concatenate(
                        [
                            d_all[j * chans:(j + 1) * chans, c * toks:(c + 1) * toks]
                            for j in range(jq)
                        ],
                        axis=1,
                    )
                    for c in range(c0, c0 + cg)
                ],
                axis=0,
            )
            wacc[c0 * chans:(c0 + cg) * chans] += jnp.dot(left, right, preferred_element_type=F32)

        @pl.when(turn)
        def _():
            forward_finish(m_now)

        @pl.when(o < early)
        def _():
            right_final_finish(o)

        @pl.when(left_turn)
        def _():
            left_final_finish(p_now)

        return carry

    early = nq - 3
    lax.fori_loop(0, nq, outer_step, 0)

    @pl.when(inner)
    def _():
        forward_start(nq - 1)
        forward_finish(nq - 1)

    left_final_start(nl // 2 - 1)
    left_final_finish(nl // 2 - 1)

    def right_last(m, carry):
        right_final_start(m)
        right_final_finish(m)
        return carry

    lax.fori_loop(early, nq, right_last, 0)

    @pl.when(inner)
    def _():
        for m in (nq - 2, nq - 1):
            for u in range(2):
                fb_copy(m, u).wait_send()

    for m in (nq - 2, nq - 1):
        mine, theirs = right_out(m)
        mine.wait()
        theirs.wait_send()
    left_out_copy(nl // 2 - 1).wait()

    def drain(q, carry):
        for m in range(n_depth - 1):
            g_copy(m, q).wait_send()
        b_copy(q).wait_send()
        fa_copy(q).wait_send()
        right_out(q)[1].wait_recv()

        @pl.when(jnp.logical_not(inner))
        def _():
            fw_copy(q).wait_send()

        return carry

    lax.fori_loop(0, nq, drain, 0)

    def drain_l(l, carry):
        for r in range(3):
            l_copy(l, r).wait_send()
        return carry

    lax.fori_loop(0, nl, drain_l, 0)


def mega_call(a2, bt, gt, w, inv, chans, toks):
    seqs, ci = a2.shape
    jh, je = gt.shape[1], bt.shape[1]
    i_own, pair_ch = gt.shape[2:]
    n_depth, n_row = lax.axis_size("depth"), lax.axis_size("row")
    nq = nl = 8
    wide = je // nq
    lw = ci // nl
    quarter = seqs // n_row
    piece = 2 * quarter
    hbm = lambda *s: jax.ShapeDtypeStruct(s, BF16)
    dma = lambda *s: pltpu.SemaphoreType.DMA(s)
    anyspec = pl.BlockSpec(memory_space=pl.ANY)
    vmem = pl.BlockSpec(memory_space=pltpu.VMEM)
    eye = jnp.eye(seqs, dtype=BF16)
    return pl.pallas_call(
        functools.partial(mega_kernel, (chans, seqs, toks, nq, nl, quarter), inv),
        out_shape=(
            hbm(nq, n_row * piece, wide),
            hbm(nq, 2 * piece, wide),
            hbm(nq, piece, wide),
            hbm(nq, piece, wide),
            hbm(nl, n_row * piece, lw),
            hbm(3, nl, piece, lw),
            hbm(je, seqs),
            hbm(quarter, 2 * je),
            jax.ShapeDtypeStruct((piece, chans, toks), F32),
            jax.ShapeDtypeStruct((chans * chans, pair_ch), F32),
        ),
        in_specs=[anyspec, anyspec, anyspec, vmem, vmem],
        out_specs=(anyspec,) * 9 + (vmem,),
        scratch_shapes=[
            pltpu.VMEM((2 * seqs, ci), BF16),
            pltpu.VMEM((je, ci), BF16),
            pltpu.VMEM((2 * seqs, je), BF16),
            pltpu.VMEM((jh, i_own * n_depth, pair_ch), BF16),
            pltpu.VMEM((2, n_row * piece, wide), BF16),
            pltpu.VMEM((2, 2, wide, seqs), BF16),
            pltpu.VMEM((2, 2 * piece, wide), BF16),
            pltpu.VMEM((2, 2 * piece, wide), BF16),
            pltpu.VMEM((piece * 8, toks), F32),
            dma(3), dma(1), dma(n_depth - 1, nq), dma(n_depth - 1, nq), dma(nq), dma(nq), dma(2),
            dma(nq), dma(nq), dma(nq), dma(nq), dma(2, nq), dma(nq),
            dma(3, nl), dma(3, nl), dma(2, 2), dma(2),
            dma(nq), dma(nq), dma(nq), dma(3), dma(2, 4), dma(1),
        ],
        compiler_params=pltpu.CompilerParams(
            vmem_limit_bytes=MEGA_VMEM, collective_id=0, has_side_effects=True
        ),
        cost_estimate=cost(6 * seqs * 2 * je * ci, 8 * seqs * ci),
        name="mega",
    )(a2, bt, gt, w, eye)


def mega_body(left_factor, right_factor, out_weight, pair_cotangent):
    seqs, chans, rows = left_factor.shape
    toks = right_factor.shape[2]
    pair_ch = out_weight.shape[1]
    inv = 1.0 / (seqs * lax.axis_size("depth"))
    jh = toks // 2
    quarter = seqs // lax.axis_size("row")

    a2 = left_factor.reshape(seqs, chans * rows)
    bt = jnp.transpose(right_factor, (2, 1, 0)).reshape(2, jh * chans, seqs)
    gt = jnp.transpose(pair_cotangent, (1, 0, 2)).reshape(2, jh, -1, pair_ch)
    *_, rfin, left_grad, wacc = mega_call(a2, bt, gt, out_weight, inv, chans, rows)

    axes = ("depth", "row", "col")
    count = lax.axis_size(axes)
    pieces = wacc.reshape(count, chans * chans // count, pair_ch)
    pieces = lax.all_to_all(pieces, axes, split_axis=0, concat_axis=0, tiled=True)

    right_grad = rfin.reshape(quarter, toks, chans)
    right_grad = jnp.transpose(right_grad, (0, 2, 1)).astype(F32)
    return left_grad, right_grad, jnp.sum(pieces, axis=0)


def plain_body(left_factor, right_factor, out_weight, pair_cotangent):
    seq_total = left_factor.shape[0] * lax.axis_size("depth")
    chans = left_factor.shape[1]
    rows_here = left_factor.shape[2]
    cols_here = right_factor.shape[2]
    width = out_weight.shape[0]
    pair_ch = out_weight.shape[1]
    natural = jnp.einsum("sci,sej->ciej", left_factor, right_factor, preferred_element_type=F32) / seq_total
    outer = jnp.transpose(natural.astype(BF16), (1, 3, 0, 2)).reshape(rows_here * cols_here, width)
    piece = lax.all_gather(pair_cotangent, "depth", axis=0, tiled=True)
    grad_two = piece.reshape(rows_here * cols_here, pair_ch)
    delta = jnp.dot(grad_two, out_weight.T, preferred_element_type=F32).astype(BF16)
    weight_acc = jnp.dot(outer.T, grad_two, preferred_element_type=F32)
    delta_four = delta.reshape(rows_here, cols_here, chans, chans)
    left_part = jnp.einsum("ijce,sej->sci", delta_four, right_factor, preferred_element_type=F32) / seq_total
    right_part = jnp.einsum("ijce,sci->sej", delta_four, left_factor, preferred_element_type=F32) / seq_total
    left_grad = lax.psum_scatter(left_part, "col", scatter_dimension=0, tiled=True)
    right_grad = lax.psum_scatter(right_part, "row", scatter_dimension=0, tiled=True)
    middle = lax.psum_scatter(weight_acc, ("depth", "row"), scatter_dimension=0, tiled=True)
    weight_grad = lax.psum_scatter(middle, "col", scatter_dimension=0, tiled=True)
    return left_grad, right_grad, weight_grad


def body(left_factor, right_factor, out_weight, pair_cotangent):
    seqs, chans, rows = left_factor.shape
    toks = right_factor.shape[2]
    fits = toks % 128 == 0 and toks <= 256 and rows % 32 == 0 and chans == 32 and seqs <= 512
    shape = tuple(lax.axis_size(x) for x in ("depth", "row", "col"))
    mega = (
        fits and shape == (4, 4, 2) and toks == 256 and rows == 128 and seqs % 64 == 0
        and out_weight.shape[1] == 128
    )
    run = mega_body if mega else fused_body if fits else plain_body
    return run(left_factor, right_factor, out_weight, pair_cotangent)


def solution(mesh):
    return jax.shard_map(
        body,
        mesh=mesh,
        in_specs=(
            P("depth", None, "row"),
            P("depth", None, "col"),
            P(),
            P(("row", "depth"), "col", None),
        ),
        out_specs=(
            P(("depth", "col"), None, "row"),
            P(("depth", "row"), None, "col"),
            P(("depth", "row", "col"), None),
        ),
        check_vma=False,
    )
```

```python
import functools

import jax
import jax.numpy as jnp
from jax import lax
from jax.experimental import pallas as pl
from jax.experimental.pallas import tpu as pltpu
from jax.sharding import PartitionSpec as P

F32 = jnp.float32
BF16 = jnp.bfloat16
VMEM_CAP = 60 * 1024 * 1024
MEGA_VMEM = 62 * 1024 * 1024
MESH = pl.DeviceIdType.MESH


def params():
    return pltpu.CompilerParams(vmem_limit_bytes=VMEM_CAP)


def cost(flops, nbytes):
    return pl.CostEstimate(flops=flops, bytes_accessed=nbytes, transcendentals=0)


def outer_kernel(inv, at_ref, b_ref, o_ref):
    width = 512 if o_ref.shape[1] % 512 == 0 else o_ref.shape[1]
    for n in range(o_ref.shape[1] // width):
        cols = slice(n * width, (n + 1) * width)
        acc = jnp.dot(at_ref[...], b_ref[:, cols], preferred_element_type=F32)
        o_ref[:, cols] = (acc * inv).astype(BF16)


def outer_call(at, b2, inv, tm, tn, part, cols):
    rows, seqs = at.shape
    first = part * cols // tn
    return pl.pallas_call(
        functools.partial(outer_kernel, inv),
        out_shape=jax.ShapeDtypeStruct((rows, cols), BF16),
        grid=(cols // tn, rows // tm),
        in_specs=[
            pl.BlockSpec((tm, seqs), lambda n, m: (m, 0)),
            pl.BlockSpec((seqs, tn), lambda n, m: (0, n + first)),
        ],
        out_specs=pl.BlockSpec((tm, tn), lambda n, m: (m, n)),
        compiler_params=params(),
        cost_estimate=cost(2 * rows * cols * seqs, 2 * rows * cols + 2 * seqs * (rows + cols)),
        name=f"outer_{part}",
    )(at, b2)


def delta_kernel(inv, chans, toks, w_ref, g_ref, a_ref, d_ref, r_ref, acc_ref):
    step = pl.program_id(0)
    here = g_ref.shape[0]
    eb = w_ref.shape[0] // chans

    def one(i, carry):
        d = lax.dot_general(
            w_ref[...], g_ref[i], (((1,), (1,)), ((), ())), preferred_element_type=F32
        ).astype(BF16)
        at = pl.multiple_of(i * chans, chans)
        for e in range(eb):
            d_ref[pl.ds(at, chans), e * toks:(e + 1) * toks] = d[e * chans:(e + 1) * chans]
        return carry

    lax.fori_loop(0, here, one, 0, unroll=8)

    @pl.when(step == 0)
    def _():
        acc_ref[...] = jnp.zeros_like(acc_ref)

    for e in range(eb):
        cols = slice(e * toks, (e + 1) * toks)
        acc_ref[:, cols] += jnp.dot(a_ref[...], d_ref[:, cols], preferred_element_type=F32)

    @pl.when(step == pl.num_programs(0) - 1)
    def _():
        r_ref[...] = (acc_ref[...] * inv).astype(BF16)


def delta_call(w_ec, g, a2, inv, chans, part, eb, ti):
    rows, toks, pair_ch = g.shape
    seqs = a2.shape[0]
    wide = eb * toks
    return pl.pallas_call(
        functools.partial(delta_kernel, inv, chans, toks),
        out_shape=(
            jax.ShapeDtypeStruct((rows * chans, wide), BF16),
            jax.ShapeDtypeStruct((seqs, wide), BF16),
        ),
        grid=(rows // ti,),
        in_specs=[
            pl.BlockSpec((eb * chans, pair_ch), lambda m: (part, 0)),
            pl.BlockSpec((ti, toks, pair_ch), lambda m: (m, 0, 0)),
            pl.BlockSpec((seqs, ti * chans), lambda m: (0, m)),
        ],
        out_specs=(
            pl.BlockSpec((ti * chans, wide), lambda m: (m, 0)),
            pl.BlockSpec((seqs, wide), lambda m: (0, 0)),
        ),
        scratch_shapes=[pltpu.VMEM((seqs, wide), F32)],
        compiler_params=params(),
        cost_estimate=cost(
            2 * rows * chans * wide * (seqs + 2 * pair_ch),
            2 * rows * (chans * wide + toks * pair_ch + chans * seqs),
        ),
        name=f"delta_right_{part}",
    )(w_ec, g, a2)


def left_kernel(inv, parts, b_ref, *refs):
    d_refs, o_ref = refs[:parts], refs[parts]
    wide = d_refs[0].shape[1]
    acc = None
    for k in range(parts):
        term = lax.dot_general(
            b_ref[:, k * wide:(k + 1) * wide],
            d_refs[k][...],
            (((1,), (1,)), ((), ())),
            preferred_element_type=F32,
        )
        acc = term if acc is None else acc + term
    o_ref[...] = (acc * inv).astype(BF16)


def left_call(b2, ds, inv, tn):
    seqs = b2.shape[0]
    rows, wide = ds[0].shape
    parts = len(ds)
    return pl.pallas_call(
        functools.partial(left_kernel, inv, parts),
        out_shape=jax.ShapeDtypeStruct((seqs, rows), BF16),
        grid=(rows // tn,),
        in_specs=[pl.BlockSpec((seqs, parts * wide), lambda m: (0, 0))]
        + [pl.BlockSpec((tn, wide), lambda m: (m, 0))] * parts,
        out_specs=pl.BlockSpec((seqs, tn), lambda m: (0, m)),
        compiler_params=params(),
        cost_estimate=cost(2 * seqs * rows * wide * parts, 2 * rows * wide * parts + 4 * seqs * rows),
        name="left",
    )(b2, *ds)


def weight_kernel(chans, *refs):
    o_refs, g_ref, w_ref = refs[:-2], refs[-2], refs[-1]
    ti, toks, pair_ch = g_ref.shape
    per = o_refs[0].shape[1] // toks

    @pl.when(pl.program_id(0) == 0)
    def _():
        w_ref[...] = jnp.zeros_like(w_ref)

    group = 4
    eg = 8 if per % 8 == 0 else 1

    def one(k, carry):
        first = pl.multiple_of(k * group, group)
        right = g_ref[pl.ds(first, group)].reshape(group * toks, pair_ch)
        for h, o_ref in enumerate(o_refs):
            for e0 in range(0, per, eg):
                left = jnp.concatenate(
                    [
                        jnp.concatenate(
                            [
                                o_ref[
                                    pl.ds(pl.multiple_of((first + i) * chans, chans), chans),
                                    e * toks:(e + 1) * toks,
                                ]
                                for i in range(group)
                            ],
                            axis=1,
                        )
                        for e in range(e0, e0 + eg)
                    ],
                    axis=0,
                )
                at = (h * per + e0) * chans
                w_ref[at:at + eg * chans] += jnp.dot(left, right, preferred_element_type=F32)
        return carry

    lax.fori_loop(0, ti // group, one, 0)


def weight_call(outers, g, chans, ti):
    rows, toks, pair_ch = g.shape
    cols = outers[0].shape[1]
    width = cols * len(outers) // toks * chans
    return pl.pallas_call(
        functools.partial(weight_kernel, chans),
        out_shape=jax.ShapeDtypeStruct((width, pair_ch), F32),
        grid=(rows // ti,),
        in_specs=[pl.BlockSpec((ti * chans, cols), lambda m: (m, 0))] * len(outers)
        + [pl.BlockSpec((ti, toks, pair_ch), lambda m: (m, 0, 0))],
        out_specs=pl.BlockSpec((width, pair_ch), lambda m: (0, 0)),
        compiler_params=params(),
        cost_estimate=cost(4 * rows * toks * width * pair_ch, 2 * rows * toks * width),
        name="weight",
    )(*outers, g)


def fused_body(left_factor, right_factor, out_weight, pair_cotangent):
    seqs, chans, rows = left_factor.shape
    toks = right_factor.shape[2]
    pair_ch = out_weight.shape[1]
    inv = 1.0 / (seqs * lax.axis_size("depth"))
    n_col = lax.axis_size("col")
    parts = 4
    eb = chans // parts

    g = lax.all_gather(pair_cotangent, "depth", axis=0, tiled=True)
    a2 = jnp.transpose(left_factor, (0, 2, 1)).reshape(seqs, rows * chans)
    at = jnp.transpose(left_factor, (2, 1, 0)).reshape(rows * chans, seqs)
    b2 = right_factor.reshape(seqs, chans * toks)
    w_ec = jnp.transpose(out_weight.reshape(chans, chans, pair_ch), (1, 0, 2)).reshape(
        chans * chans, pair_ch
    )

    half_cols = b2.shape[1] // 2
    outer_a = outer_call(at, b2, inv, 16 * chans, eb * toks, 0, half_cols)
    g, outer_a = lax.optimization_barrier((g, outer_a))

    ds, rights = [], []
    for k in range(parts):
        d, r = delta_call(w_ec, g, a2, inv, chans, k, eb, 32)
        ds.append(d)
        r, g = lax.optimization_barrier((r, g))
        rights.append(lax.psum_scatter(r, "row", scatter_dimension=0, tiled=True))
    left = left_call(b2, ds, inv, 8 * chans)
    left, at, b2 = lax.optimization_barrier((left, at, b2))
    if n_col == 2:
        half = seqs // 2
        me = lax.axis_index("col")
        mine = lax.dynamic_slice_in_dim(left, me * half, half, 0)
        theirs = lax.dynamic_slice_in_dim(left, (1 - me) * half, half, 0)
        theirs, at, b2 = lax.optimization_barrier((theirs, at, b2))
        got = lax.ppermute(theirs, "col", [(0, 1), (1, 0)])
        left_grad = mine.astype(F32) + got.astype(F32)
    else:
        left_grad = lax.psum_scatter(left, "col", scatter_dimension=0, tiled=True).astype(F32)
    left_grad = jnp.transpose(left_grad.reshape(-1, rows, chans), (0, 2, 1))
    outer_b = outer_call(at, b2, inv, 16 * chans, eb * toks, 1, half_cols)
    weight_acc = weight_call((outer_a, outer_b), g, chans, 8)
    weight_acc = jnp.transpose(weight_acc.reshape(chans, chans, pair_ch), (1, 0, 2)).reshape(
        chans * chans, pair_ch
    )
    axes = ("depth", "row", "col")
    count = lax.axis_size(axes)
    pieces = weight_acc.reshape(count, chans * chans // count, pair_ch)
    pieces = lax.all_to_all(pieces, axes, split_axis=0, concat_axis=0, tiled=True)
    rights = [r.reshape(-1, eb, toks) for r in rights]
    right_grad = jnp.concatenate(rights, axis=1).astype(F32)
    pieces, left_grad, right_grad = lax.optimization_barrier((pieces, left_grad, right_grad))
    weight_grad = jnp.sum(pieces, axis=0)
    return left_grad, right_grad, weight_grad


def mega_kernel(
    dims, inv, a_hbm, bt_hbm, g_hbm, w_ref, eye_ref,
    rown, rfw, rfa, rfb, lown, lrecv, btr, rfin, left_out, w_out,
    a_all, d_all, b_all, g_all, stage, btc, fin, fsum, lbuf,
    wacc, w1s, w1r, w2s, w2r, w3s, w3r,
    a_sem, g_loc, g_s, g_r, b_s, b_r, st_sem, fa_s, fa_r, fw_s, fw_r, fb_s, fb_r,
    l_s, l_r, btc_sem, fin_sem, rx_s, rx_r, rx_l, rl_sem, ll_sem, lo_sem,
    w1_s, w1_q, w2_s, w2_q, w3_sem,
):
    chans, seqs, toks, nq, nl, quarter = dims
    n_depth, n_row, n_col = (lax.axis_size(x) for x in ("depth", "row", "col"))
    depth, row, col = (lax.axis_index(x) for x in ("depth", "row", "col"))
    core = lax.rem(depth, 2)
    buddy = depth + 1 - 2 * core
    pair = row + 1 - 2 * lax.rem(row, 2)
    far = 2 - 2 * (row // 2)
    inner = jnp.logical_or(row == 1, row == 2)
    jq = g_all.shape[0] // nq
    wide = jq * chans
    i_own = g_hbm.shape[2]
    lw = a_all.shape[1] // nl

    def remote(src, dst, ss, rs, **where):
        return pltpu.make_async_remote_copy(
            src_ref=src, dst_ref=dst, send_sem=ss, recv_sem=rs,
            device_id=where, device_id_type=MESH,
        )

    barrier = pltpu.get_barrier_semaphore()
    peers = [{"depth": lax.rem(depth + m, n_depth)} for m in range(1, n_depth)]
    peers += [{"row": lax.rem(row + m, n_row)} for m in range(1, n_row)]
    peers += [{"col": 1 - col}, {"depth": buddy, "col": 1 - col}]
    for where in peers:
        pl.semaphore_signal(barrier, inc=1, device_id=where, device_id_type=MESH)
    pl.semaphore_wait(barrier, len(peers))

    def g_copy(m, q):
        to = lax.rem(depth + m + 1, n_depth)
        js = pl.ds(pl.multiple_of(q * jq, jq), jq)
        rows = pl.ds(pl.multiple_of(depth * i_own, i_own), i_own)
        return remote(
            g_hbm.at[lax.rem(to, 2), js], g_all.at[js, rows], g_s.at[m, q], g_r.at[m, q], depth=to
        )

    def b_copy(q):
        rows = pl.ds(pl.multiple_of(q * wide, wide), wide)
        return remote(bt_hbm.at[1 - core, rows], btr.at[rows], b_s.at[q], b_r.at[q], depth=buddy)

    own_rows = pl.ds(pl.multiple_of(core * seqs, seqs), seqs)
    a_local = pltpu.make_async_copy(a_hbm, a_all.at[own_rows], a_sem.at[0])
    a_remote = remote(a_hbm, a_all.at[own_rows], a_sem.at[1], a_sem.at[2], depth=buddy)
    g_local = pltpu.make_async_copy(
        g_hbm.at[core], g_all.at[:, pl.ds(pl.multiple_of(depth * i_own, i_own), i_own)], g_loc.at[0]
    )
    for m in range(n_depth - 1):
        g_copy(m, 0).start()
    a_remote.start()
    g_local.start()
    a_local.start()

    def send_rest(q, carry):
        for m in range(n_depth - 1):
            g_copy(m, q).start()
        return carry

    lax.fori_loop(1, nq, send_rest, 0)

    def send_b(q, carry):
        b_copy(q).start()
        return carry

    lax.fori_loop(0, nq, send_b, 0)
    g_local.wait()

    def bt_load(q, slot):
        rows = pl.ds(pl.multiple_of(q * wide, wide), wide)
        return (
            pltpu.make_async_copy(bt_hbm.at[core, rows], btc.at[slot, core], btc_sem.at[slot, 0]),
            pltpu.make_async_copy(btr.at[rows], btc.at[slot, 1 - core], btc_sem.at[slot, 1]),
        )

    def build_b(q):
        for cp in bt_load(q, 0):
            cp.wait()
        cols = pl.ds(pl.multiple_of(q * wide, wide), wide)
        for h in range(2):
            b_all[h * seqs:(h + 1) * seqs, cols] = lax.dot_general(
                eye_ref[...], btc[0, h], (((1,), (1,)), ((), ())), preferred_element_type=F32
            ).astype(BF16)

    piece = 2 * quarter

    def target(t, count):
        return pl.ds(pl.multiple_of(t * piece, piece), count * piece)

    def fa_copy(q):
        return remote(
            rown.at[q, target(pair, 1)], rfa.at[q], fa_s.at[q], fa_r.at[q], row=pair
        )

    def fw_copy(q):
        return remote(
            rown.at[q, target(far, 2)], rfw.at[q], fw_s.at[q], fw_r.at[q], row=pair
        )

    def fb_copy(m, u):
        return remote(
            fsum.at[lax.rem(m, 2), u * piece:(u + 1) * piece], rfb.at[m], fb_s.at[u, m], fb_r.at[m], row=far + u
        )

    def fin_loads(m):
        return (
            pltpu.make_async_copy(rfw.at[m], fin.at[0], fin_sem.at[0]),
            pltpu.make_async_copy(rown.at[m, target(far, 2)], fin.at[1], fin_sem.at[1]),
        )

    def forward_start(m):
        fw_copy(m).wait_recv()
        for cp in fin_loads(m):
            cp.start()

    def forward_finish(m):
        for cp in fin_loads(m):
            cp.wait()

        @pl.when(m >= 2)
        def _():
            for u in range(2):
                fb_copy(m - 2, u).wait_send()

        fsum[lax.rem(m, 2)] = (fin[0].astype(F32) + fin[1].astype(F32)).astype(BF16)
        for u in range(2):
            fb_copy(m, u).start()

    def right_step(q, carry):
        turn = jnp.logical_and(inner, jnp.logical_and(q >= 3, lax.rem(q, 2) == 1))
        m_now = jnp.maximum((q - 3) // 2, 0)

        @pl.when(turn)
        def _():
            forward_start(m_now)

        for m in range(n_depth - 1):
            g_copy(m, q).wait_recv()
        rows = pl.multiple_of(q * wide, wide)
        for u in range(jq // 2):
            pair_g = g_all[pl.ds(q * jq + 2 * u, 2)].reshape(2 * toks, -1)
            d = lax.dot_general(
                w_ref[...], pair_g, (((1,), (1,)), ((), ())), preferred_element_type=F32
            ).astype(BF16)
            for v in range(2):
                at = pl.multiple_of(rows + (2 * u + v) * chans, chans)
                for c in range(chans):
                    d_all[pl.ds(at, chans), c * toks:(c + 1) * toks] = d[
                        c * chans:(c + 1) * chans, v * toks:(v + 1) * toks
                    ]

        @pl.when(q == 0)
        def _():
            a_local.wait()
            a_remote.wait()

        half = wide // 2
        for n in range(2):
            at = pl.multiple_of(rows + n * half, half)
            r = lax.dot_general(
                a_all[...], d_all[pl.ds(at, half)], (((1,), (1,)), ((), ())), preferred_element_type=F32
            )
            r = (r * inv).astype(BF16)
            for h in range(2):
                for t in range(n_row):
                    first = h * seqs + t * quarter
                    at = t * piece + h * quarter
                    stage[0, at:at + quarter, n * half:(n + 1) * half] = r[first:first + quarter]
        out = pltpu.make_async_copy(stage.at[0], rown.at[q], st_sem.at[0])
        out.start()

        @pl.when(q > 0)
        def _():
            build_b(q - 1)

        b_copy(q).wait_recv()
        for cp in bt_load(q, 0):
            cp.start()
        out.wait()

        @pl.when(jnp.logical_not(inner))
        def _():
            fw_copy(q).start()

        fa_copy(q).start()

        @pl.when(turn)
        def _():
            forward_finish(m_now)

        return carry

    lax.fori_loop(0, nq, right_step, 0)
    build_b(nq - 1)

    def l_copy(l, r):
        kk = core if r == 1 else 1 - core
        tx = col if r == 0 else 1 - col
        where = ({"depth": buddy}, {"col": 1 - col}, {"depth": buddy, "col": 1 - col})[r]
        return remote(
            lown.at[l, target(kk * 2 + tx, 1)], lrecv.at[r, l], l_s.at[r, l], l_r.at[r, l], **where
        )

    def l_out(l):
        slot = lax.rem(l, 2)
        return pltpu.make_async_copy(stage.at[slot], lown.at[l], st_sem.at[slot])

    def l_send(l):
        l_out(l).wait()
        for r in (2, 1, 0):
            l_copy(l, r).start()

    def left_step(l, carry):
        turn = jnp.logical_and(inner, lax.rem(l, 3) == 1)
        m_now = 3 + l // 3

        @pl.when(turn)
        def _():
            forward_start(m_now)

        half = lw // 2
        slot = lax.rem(l, 2)
        for n in range(2):
            cols = pl.ds(pl.multiple_of(l * lw + n * half, half), half)
            x = jnp.dot(b_all[...], d_all[:, cols], preferred_element_type=F32)
            x = (x * inv).astype(BF16)
            stage[slot, :, n * half:(n + 1) * half] = x
        l_out(l).start()

        @pl.when(l > 0)
        def _():
            l_send(l - 1)

        @pl.when(turn)
        def _():
            forward_finish(m_now)

        return carry

    for cp in bt_load(0, 0):
        cp.start()
    lax.fori_loop(0, nl, left_step, 0)
    l_send(nl - 1)

    wacc[...] = jnp.zeros_like(wacc)

    def right_loads(m):
        srcs = (rown.at[m, target(row, 1)], rfa.at[m], rfb.at[m])
        return [
            pltpu.make_async_copy(
                src, b_all.at[n * piece:(n + 1) * piece, 7 * wide:8 * wide], rl_sem.at[n]
            )
            for n, src in enumerate(srcs)
        ]

    def right_out(m, sent=False):
        slot = lax.rem(m, 2)
        cols = pl.ds(pl.multiple_of((core * nq + m) * wide, wide), wide)

        def rows(k):
            at = slot * piece + k * quarter
            return b_all.at[pl.ds(pl.multiple_of(at, quarter), quarter), 6 * wide:7 * wide]

        away = remote(rows(1 - core), rfin.at[:, cols], rx_s.at[m], rx_r.at[m], depth=buddy)
        if sent:
            return away
        return pltpu.make_async_copy(rows(core), rfin.at[:, cols], rx_l.at[m]), away

    def right_final_start(m):
        fa_copy(m).wait_recv()
        fb_copy(m, 0).wait_recv()
        for cp in right_loads(m):
            cp.start()

    def right_final_finish(m):
        for cp in right_loads(m):
            cp.wait()

        @pl.when(m >= 2)
        def _():
            mine, theirs = right_out(m - 2)
            mine.wait()
            theirs.wait_send()

        total = sum(
            b_all[n * piece:(n + 1) * piece, 7 * wide:8 * wide].astype(F32) for n in range(3)
        ).astype(BF16)
        at = pl.multiple_of(lax.rem(m, 2) * piece, piece)
        b_all[pl.ds(at, piece), 6 * wide:7 * wide] = total
        for cp in right_out(m):
            cp.start()

    def left_loads(p):
        cps = []
        for h in range(2):
            l = 2 * p + h
            srcs = [lown.at[l, target(core * 2 + col, 1)]] + [lrecv.at[r, l] for r in range(3)]
            for n, src in enumerate(srcs):
                dst = b_all.at[n * piece:(n + 1) * piece, h * lw:(h + 1) * lw]
                cps.append(pltpu.make_async_copy(src, dst, ll_sem.at[h, n]))
        return cps

    def left_out_copy(p):
        cs = pl.ds(pl.multiple_of(p * 8, 8), 8)
        return pltpu.make_async_copy(lbuf.reshape(piece, 8, toks), left_out.at[:, cs], lo_sem.at[0])

    def left_final_start(p):
        for h in range(2):
            for r in range(3):
                l_copy(2 * p + h, r).wait_recv()
        for cp in left_loads(p):
            cp.start()

    def left_final_finish(p):
        for cp in left_loads(p):
            cp.wait()

        @pl.when(p >= 1)
        def _():
            left_out_copy(p - 1).wait()

        for h in range(2):
            for c in range(4):
                cols = slice(h * lw + c * toks, h * lw + (c + 1) * toks)
                lbuf[pl.ds(4 * h + c, piece, stride=8), :] = sum(
                    b_all[n * piece:(n + 1) * piece, cols].astype(F32) for n in range(4)
                )
        left_out_copy(p).start()

    def outer_step(o, carry):
        left_turn = lax.rem(o, 3) == 0
        turn = jnp.logical_and(inner, jnp.logical_and(o > 0, left_turn))
        m_now = 5 + o // 3
        p_now = o // 3

        @pl.when(turn)
        def _():
            forward_start(m_now)

        @pl.when(o < early)
        def _():
            right_final_start(o)

        @pl.when(left_turn)
        def _():
            left_final_start(p_now)

        slot = lax.rem(o, 2)
        for cp in bt_load(o, slot):
            cp.wait()

        @pl.when(o < nq - 1)
        def _():
            for cp in bt_load(o + 1, 1 - slot):
                cp.start()

        width = 512
        for n in range(a_all.shape[1] // width):
            cols = slice(n * width, (n + 1) * width)
            x = jnp.dot(btc[slot, 0], a_all[:seqs, cols], preferred_element_type=F32)
            x += jnp.dot(btc[slot, 1], a_all[seqs:, cols], preferred_element_type=F32)
            d_all[:wide, cols] = (x * inv).astype(BF16)
        right = g_all[pl.ds(pl.multiple_of(o * jq, jq), jq)].reshape(jq * toks, -1)
        cg = 8
        for c0 in range(0, chans, cg):
            left = jnp.concatenate(
                [
                    jnp.concatenate(
                        [
                            d_all[j * chans:(j + 1) * chans, c * toks:(c + 1) * toks]
                            for j in range(jq)
                        ],
                        axis=1,
                    )
                    for c in range(c0, c0 + cg)
                ],
                axis=0,
            )
            wacc[c0 * chans:(c0 + cg) * chans] += jnp.dot(left, right, preferred_element_type=F32)

        @pl.when(turn)
        def _():
            forward_finish(m_now)

        @pl.when(o < early)
        def _():
            right_final_finish(o)

        @pl.when(left_turn)
        def _():
            left_final_finish(p_now)

        return carry

    early = nq - 1
    lax.fori_loop(0, nq, outer_step, 0)

    n1 = wacc.shape[0] // n_depth
    n2 = n1 // n_row
    n3 = n2 // 2

    def part(ref, index, size):
        return ref.at[pl.ds(pl.multiple_of(index * size, size), size)]

    def w1_copy(m):
        to = lax.rem(depth + m + 1, n_depth)
        return remote(part(w1s, to, n1), w1r.at[m], w1_s.at[m], w1_q.at[m], depth=to)

    def w2_copy(m):
        to = lax.rem(row + m + 1, n_row)
        return remote(part(w2s, to, n2), w2r.at[m], w2_s.at[m], w2_q.at[m], row=to)

    w3_copy = remote(part(w3s, 1 - col, n3), w3r, w3_sem.at[0], w3_sem.at[1], col=1 - col)

    w1s[...] = wacc[...].astype(BF16)
    for m in range(n_depth - 1):
        w1_copy(m).start()
    left_final_start(nl // 2 - 1)
    left_final_finish(nl // 2 - 1)
    for m in range(n_depth - 1):
        w1_copy(m).wait()
    w2s[...] = part(wacc, depth, n1)[...] + sum(w1r[m].astype(F32) for m in range(n_depth - 1))
    for m in range(n_row - 1):
        w2_copy(m).start()
    right_final_start(nq - 1)
    right_final_finish(nq - 1)
    for m in range(n_row - 1):
        w2_copy(m).wait()
    w3s[...] = part(w2s, row, n2)[...] + sum(w2r[m] for m in range(n_row - 1))
    w3_copy.start()

    @pl.when(inner)
    def _():
        for m in (nq - 2, nq - 1):
            for u in range(2):
                fb_copy(m, u).wait_send()

    for m in (nq - 2, nq - 1):
        mine, theirs = right_out(m)
        mine.wait()
        theirs.wait_send()
    left_out_copy(nl // 2 - 1).wait()

    def drain(q, carry):
        for m in range(n_depth - 1):
            g_copy(m, q).wait_send()
        b_copy(q).wait_send()
        fa_copy(q).wait_send()
        right_out(q, True).wait_recv()

        @pl.when(jnp.logical_not(inner))
        def _():
            fw_copy(q).wait_send()

        return carry

    lax.fori_loop(0, nq, drain, 0)

    def drain_l(l, carry):
        for r in range(3):
            l_copy(l, r).wait_send()
        return carry

    lax.fori_loop(0, nl, drain_l, 0)
    w3_copy.wait()
    w_out[...] = part(w3s, col, n3)[...] + w3r[...]


def mega_call(a2, bt, gt, w, inv, chans, toks):
    seqs, ci = a2.shape
    jh, je = gt.shape[1], bt.shape[1]
    i_own, pair_ch = gt.shape[2:]
    n_depth, n_row = lax.axis_size("depth"), lax.axis_size("row")
    nq = nl = 8
    wide = je // nq
    lw = ci // nl
    quarter = seqs // n_row
    piece = 2 * quarter
    n1 = chans * chans // n_depth
    n2 = n1 // n_row
    n3 = n2 // 2
    hbm = lambda *s: jax.ShapeDtypeStruct(s, BF16)
    dma = lambda *s: pltpu.SemaphoreType.DMA(s)
    anyspec = pl.BlockSpec(memory_space=pl.ANY)
    vmem = pl.BlockSpec(memory_space=pltpu.VMEM)
    eye = jnp.eye(seqs, dtype=BF16)
    return pl.pallas_call(
        functools.partial(mega_kernel, (chans, seqs, toks, nq, nl, quarter), inv),
        out_shape=(
            hbm(nq, n_row * piece, wide),
            hbm(nq, 2 * piece, wide),
            hbm(nq, piece, wide),
            hbm(nq, piece, wide),
            hbm(nl, n_row * piece, lw),
            hbm(3, nl, piece, lw),
            hbm(je, seqs),
            hbm(quarter, 2 * je),
            jax.ShapeDtypeStruct((piece, chans, toks), F32),
            jax.ShapeDtypeStruct((n3, pair_ch), F32),
        ),
        in_specs=[anyspec, anyspec, anyspec, vmem, vmem],
        out_specs=(anyspec,) * 9 + (vmem,),
        scratch_shapes=[
            pltpu.VMEM((2 * seqs, ci), BF16),
            pltpu.VMEM((je, ci), BF16),
            pltpu.VMEM((2 * seqs, je), BF16),
            pltpu.VMEM((jh, i_own * n_depth, pair_ch), BF16),
            pltpu.VMEM((2, n_row * piece, wide), BF16),
            pltpu.VMEM((2, 2, wide, seqs), BF16),
            pltpu.VMEM((2, 2 * piece, wide), BF16),
            pltpu.VMEM((2, 2 * piece, wide), BF16),
            pltpu.VMEM((piece * 8, toks), F32),
            pltpu.VMEM((chans * chans, pair_ch), F32),
            pltpu.VMEM((chans * chans, pair_ch), BF16),
            pltpu.VMEM((n_depth - 1, n1, pair_ch), BF16),
            pltpu.VMEM((n1, pair_ch), F32),
            pltpu.VMEM((n_row - 1, n2, pair_ch), F32),
            pltpu.VMEM((n2, pair_ch), F32),
            pltpu.VMEM((n3, pair_ch), F32),
            dma(3), dma(1), dma(n_depth - 1, nq), dma(n_depth - 1, nq), dma(nq), dma(nq), dma(2),
            dma(nq), dma(nq), dma(nq), dma(nq), dma(2, nq), dma(nq),
            dma(3, nl), dma(3, nl), dma(2, 2), dma(2),
            dma(nq), dma(nq), dma(nq), dma(3), dma(2, 4), dma(1),
            dma(n_depth - 1), dma(n_depth - 1), dma(n_row - 1), dma(n_row - 1), dma(2),
        ],
        compiler_params=pltpu.CompilerParams(
            vmem_limit_bytes=MEGA_VMEM, collective_id=0, has_side_effects=True
        ),
        cost_estimate=cost(6 * seqs * 2 * je * ci, 8 * seqs * ci),
        name="mega",
    )(a2, bt, gt, w, eye)


def mega_body(left_factor, right_factor, out_weight, pair_cotangent):
    seqs, chans, rows = left_factor.shape
    toks = right_factor.shape[2]
    pair_ch = out_weight.shape[1]
    inv = 1.0 / (seqs * lax.axis_size("depth"))
    jh = toks // 2
    quarter = seqs // lax.axis_size("row")

    a2 = left_factor.reshape(seqs, chans * rows)
    bt = jnp.transpose(right_factor, (2, 1, 0)).reshape(2, jh * chans, seqs)
    gt = jnp.transpose(pair_cotangent, (1, 0, 2)).reshape(2, jh, -1, pair_ch)
    *_, rfin, left_grad, weight_grad = mega_call(a2, bt, gt, out_weight, inv, chans, rows)

    right_grad = rfin.reshape(quarter, toks, chans)
    right_grad = jnp.transpose(right_grad, (0, 2, 1)).astype(F32)
    return left_grad, right_grad, weight_grad


def plain_body(left_factor, right_factor, out_weight, pair_cotangent):
    seq_total = left_factor.shape[0] * lax.axis_size("depth")
    chans = left_factor.shape[1]
    rows_here = left_factor.shape[2]
    cols_here = right_factor.shape[2]
    width = out_weight.shape[0]
    pair_ch = out_weight.shape[1]
    natural = jnp.einsum("sci,sej->ciej", left_factor, right_factor, preferred_element_type=F32) / seq_total
    outer = jnp.transpose(natural.astype(BF16), (1, 3, 0, 2)).reshape(rows_here * cols_here, width)
    piece = lax.all_gather(pair_cotangent, "depth", axis=0, tiled=True)
    grad_two = piece.reshape(rows_here * cols_here, pair_ch)
    delta = jnp.dot(grad_two, out_weight.T, preferred_element_type=F32).astype(BF16)
    weight_acc = jnp.dot(outer.T, grad_two, preferred_element_type=F32)
    delta_four = delta.reshape(rows_here, cols_here, chans, chans)
    left_part = jnp.einsum("ijce,sej->sci", delta_four, right_factor, preferred_element_type=F32) / seq_total
    right_part = jnp.einsum("ijce,sci->sej", delta_four, left_factor, preferred_element_type=F32) / seq_total
    left_grad = lax.psum_scatter(left_part, "col", scatter_dimension=0, tiled=True)
    right_grad = lax.psum_scatter(right_part, "row", scatter_dimension=0, tiled=True)
    middle = lax.psum_scatter(weight_acc, ("depth", "row"), scatter_dimension=0, tiled=True)
    weight_grad = lax.psum_scatter(middle, "col", scatter_dimension=0, tiled=True)
    return left_grad, right_grad, weight_grad


def body(left_factor, right_factor, out_weight, pair_cotangent):
    seqs, chans, rows = left_factor.shape
    toks = right_factor.shape[2]
    fits = toks % 128 == 0 and toks <= 256 and rows % 32 == 0 and chans == 32 and seqs <= 512
    shape = tuple(lax.axis_size(x) for x in ("depth", "row", "col"))
    mega = (
        fits and shape == (4, 4, 2) and toks == 256 and rows == 128 and seqs % 64 == 0
        and out_weight.shape[1] == 128
    )
    run = mega_body if mega else fused_body if fits else plain_body
    return run(left_factor, right_factor, out_weight, pair_cotangent)


def solution(mesh):
    return jax.shard_map(
        body,
        mesh=mesh,
        in_specs=(
            P("depth", None, "row"),
            P("depth", None, "col"),
            P(),
            P(("row", "depth"), "col", None),
        ),
        out_specs=(
            P(("depth", "col"), None, "row"),
            P(("depth", "row"), None, "col"),
            P(("depth", "row", "col"), None),
        ),
        check_vma=False,
    )
```

```python
import functools

import jax
import jax.numpy as jnp
from jax import lax
from jax.experimental import pallas as pl
from jax.experimental.pallas import tpu as pltpu
from jax.sharding import PartitionSpec as P

F32 = jnp.float32
BF16 = jnp.bfloat16
VMEM_CAP = 60 * 1024 * 1024
MEGA_VMEM = 62 * 1024 * 1024
MESH = pl.DeviceIdType.MESH


def params():
    return pltpu.CompilerParams(vmem_limit_bytes=VMEM_CAP)


def cost(flops, nbytes):
    return pl.CostEstimate(flops=flops, bytes_accessed=nbytes, transcendentals=0)


def outer_kernel(inv, at_ref, b_ref, o_ref):
    width = 512 if o_ref.shape[1] % 512 == 0 else o_ref.shape[1]
    for n in range(o_ref.shape[1] // width):
        cols = slice(n * width, (n + 1) * width)
        acc = jnp.dot(at_ref[...], b_ref[:, cols], preferred_element_type=F32)
        o_ref[:, cols] = (acc * inv).astype(BF16)


def outer_call(at, b2, inv, tm, tn, part, cols):
    rows, seqs = at.shape
    first = part * cols // tn
    return pl.pallas_call(
        functools.partial(outer_kernel, inv),
        out_shape=jax.ShapeDtypeStruct((rows, cols), BF16),
        grid=(cols // tn, rows // tm),
        in_specs=[
            pl.BlockSpec((tm, seqs), lambda n, m: (m, 0)),
            pl.BlockSpec((seqs, tn), lambda n, m: (0, n + first)),
        ],
        out_specs=pl.BlockSpec((tm, tn), lambda n, m: (m, n)),
        compiler_params=params(),
        cost_estimate=cost(2 * rows * cols * seqs, 2 * rows * cols + 2 * seqs * (rows + cols)),
        name=f"outer_{part}",
    )(at, b2)


def delta_kernel(inv, chans, toks, w_ref, g_ref, a_ref, d_ref, r_ref, acc_ref):
    step = pl.program_id(0)
    here = g_ref.shape[0]
    eb = w_ref.shape[0] // chans

    def one(i, carry):
        d = lax.dot_general(
            w_ref[...], g_ref[i], (((1,), (1,)), ((), ())), preferred_element_type=F32
        ).astype(BF16)
        at = pl.multiple_of(i * chans, chans)
        for e in range(eb):
            d_ref[pl.ds(at, chans), e * toks:(e + 1) * toks] = d[e * chans:(e + 1) * chans]
        return carry

    lax.fori_loop(0, here, one, 0, unroll=8)

    @pl.when(step == 0)
    def _():
        acc_ref[...] = jnp.zeros_like(acc_ref)

    for e in range(eb):
        cols = slice(e * toks, (e + 1) * toks)
        acc_ref[:, cols] += jnp.dot(a_ref[...], d_ref[:, cols], preferred_element_type=F32)

    @pl.when(step == pl.num_programs(0) - 1)
    def _():
        r_ref[...] = (acc_ref[...] * inv).astype(BF16)


def delta_call(w_ec, g, a2, inv, chans, part, eb, ti):
    rows, toks, pair_ch = g.shape
    seqs = a2.shape[0]
    wide = eb * toks
    return pl.pallas_call(
        functools.partial(delta_kernel, inv, chans, toks),
        out_shape=(
            jax.ShapeDtypeStruct((rows * chans, wide), BF16),
            jax.ShapeDtypeStruct((seqs, wide), BF16),
        ),
        grid=(rows // ti,),
        in_specs=[
            pl.BlockSpec((eb * chans, pair_ch), lambda m: (part, 0)),
            pl.BlockSpec((ti, toks, pair_ch), lambda m: (m, 0, 0)),
            pl.BlockSpec((seqs, ti * chans), lambda m: (0, m)),
        ],
        out_specs=(
            pl.BlockSpec((ti * chans, wide), lambda m: (m, 0)),
            pl.BlockSpec((seqs, wide), lambda m: (0, 0)),
        ),
        scratch_shapes=[pltpu.VMEM((seqs, wide), F32)],
        compiler_params=params(),
        cost_estimate=cost(
            2 * rows * chans * wide * (seqs + 2 * pair_ch),
            2 * rows * (chans * wide + toks * pair_ch + chans * seqs),
        ),
        name=f"delta_right_{part}",
    )(w_ec, g, a2)


def left_kernel(inv, parts, b_ref, *refs):
    d_refs, o_ref = refs[:parts], refs[parts]
    wide = d_refs[0].shape[1]
    acc = None
    for k in range(parts):
        term = lax.dot_general(
            b_ref[:, k * wide:(k + 1) * wide],
            d_refs[k][...],
            (((1,), (1,)), ((), ())),
            preferred_element_type=F32,
        )
        acc = term if acc is None else acc + term
    o_ref[...] = (acc * inv).astype(BF16)


def left_call(b2, ds, inv, tn):
    seqs = b2.shape[0]
    rows, wide = ds[0].shape
    parts = len(ds)
    return pl.pallas_call(
        functools.partial(left_kernel, inv, parts),
        out_shape=jax.ShapeDtypeStruct((seqs, rows), BF16),
        grid=(rows // tn,),
        in_specs=[pl.BlockSpec((seqs, parts * wide), lambda m: (0, 0))]
        + [pl.BlockSpec((tn, wide), lambda m: (m, 0))] * parts,
        out_specs=pl.BlockSpec((seqs, tn), lambda m: (0, m)),
        compiler_params=params(),
        cost_estimate=cost(2 * seqs * rows * wide * parts, 2 * rows * wide * parts + 4 * seqs * rows),
        name="left",
    )(b2, *ds)


def weight_kernel(chans, *refs):
    o_refs, g_ref, w_ref = refs[:-2], refs[-2], refs[-1]
    ti, toks, pair_ch = g_ref.shape
    per = o_refs[0].shape[1] // toks

    @pl.when(pl.program_id(0) == 0)
    def _():
        w_ref[...] = jnp.zeros_like(w_ref)

    group = 4
    eg = 8 if per % 8 == 0 else 1

    def one(k, carry):
        first = pl.multiple_of(k * group, group)
        right = g_ref[pl.ds(first, group)].reshape(group * toks, pair_ch)
        for h, o_ref in enumerate(o_refs):
            for e0 in range(0, per, eg):
                left = jnp.concatenate(
                    [
                        jnp.concatenate(
                            [
                                o_ref[
                                    pl.ds(pl.multiple_of((first + i) * chans, chans), chans),
                                    e * toks:(e + 1) * toks,
                                ]
                                for i in range(group)
                            ],
                            axis=1,
                        )
                        for e in range(e0, e0 + eg)
                    ],
                    axis=0,
                )
                at = (h * per + e0) * chans
                w_ref[at:at + eg * chans] += jnp.dot(left, right, preferred_element_type=F32)
        return carry

    lax.fori_loop(0, ti // group, one, 0)


def weight_call(outers, g, chans, ti):
    rows, toks, pair_ch = g.shape
    cols = outers[0].shape[1]
    width = cols * len(outers) // toks * chans
    return pl.pallas_call(
        functools.partial(weight_kernel, chans),
        out_shape=jax.ShapeDtypeStruct((width, pair_ch), F32),
        grid=(rows // ti,),
        in_specs=[pl.BlockSpec((ti * chans, cols), lambda m: (m, 0))] * len(outers)
        + [pl.BlockSpec((ti, toks, pair_ch), lambda m: (m, 0, 0))],
        out_specs=pl.BlockSpec((width, pair_ch), lambda m: (0, 0)),
        compiler_params=params(),
        cost_estimate=cost(4 * rows * toks * width * pair_ch, 2 * rows * toks * width),
        name="weight",
    )(*outers, g)


def fused_body(left_factor, right_factor, out_weight, pair_cotangent):
    seqs, chans, rows = left_factor.shape
    toks = right_factor.shape[2]
    pair_ch = out_weight.shape[1]
    inv = 1.0 / (seqs * lax.axis_size("depth"))
    n_col = lax.axis_size("col")
    parts = 4
    eb = chans // parts

    g = lax.all_gather(pair_cotangent, "depth", axis=0, tiled=True)
    a2 = jnp.transpose(left_factor, (0, 2, 1)).reshape(seqs, rows * chans)
    at = jnp.transpose(left_factor, (2, 1, 0)).reshape(rows * chans, seqs)
    b2 = right_factor.reshape(seqs, chans * toks)
    w_ec = jnp.transpose(out_weight.reshape(chans, chans, pair_ch), (1, 0, 2)).reshape(
        chans * chans, pair_ch
    )

    half_cols = b2.shape[1] // 2
    outer_a = outer_call(at, b2, inv, 16 * chans, eb * toks, 0, half_cols)
    g, outer_a = lax.optimization_barrier((g, outer_a))

    ds, rights = [], []
    for k in range(parts):
        d, r = delta_call(w_ec, g, a2, inv, chans, k, eb, 32)
        ds.append(d)
        r, g = lax.optimization_barrier((r, g))
        rights.append(lax.psum_scatter(r, "row", scatter_dimension=0, tiled=True))
    left = left_call(b2, ds, inv, 8 * chans)
    left, at, b2 = lax.optimization_barrier((left, at, b2))
    if n_col == 2:
        half = seqs // 2
        me = lax.axis_index("col")
        mine = lax.dynamic_slice_in_dim(left, me * half, half, 0)
        theirs = lax.dynamic_slice_in_dim(left, (1 - me) * half, half, 0)
        theirs, at, b2 = lax.optimization_barrier((theirs, at, b2))
        got = lax.ppermute(theirs, "col", [(0, 1), (1, 0)])
        left_grad = mine.astype(F32) + got.astype(F32)
    else:
        left_grad = lax.psum_scatter(left, "col", scatter_dimension=0, tiled=True).astype(F32)
    left_grad = jnp.transpose(left_grad.reshape(-1, rows, chans), (0, 2, 1))
    outer_b = outer_call(at, b2, inv, 16 * chans, eb * toks, 1, half_cols)
    weight_acc = weight_call((outer_a, outer_b), g, chans, 8)
    weight_acc = jnp.transpose(weight_acc.reshape(chans, chans, pair_ch), (1, 0, 2)).reshape(
        chans * chans, pair_ch
    )
    axes = ("depth", "row", "col")
    count = lax.axis_size(axes)
    pieces = weight_acc.reshape(count, chans * chans // count, pair_ch)
    pieces = lax.all_to_all(pieces, axes, split_axis=0, concat_axis=0, tiled=True)
    rights = [r.reshape(-1, eb, toks) for r in rights]
    right_grad = jnp.concatenate(rights, axis=1).astype(F32)
    pieces, left_grad, right_grad = lax.optimization_barrier((pieces, left_grad, right_grad))
    weight_grad = jnp.sum(pieces, axis=0)
    return left_grad, right_grad, weight_grad


def mega_kernel(
    dims, inv, a_hbm, bt_hbm, g_hbm, w_ref, eye_ref,
    rown, rfw, rfa, rfb, lown, lrecv, btr, rfin, left_out, w_out,
    a_all, d_all, b_all, g_all, stage, btc, fin, fsum, lbuf,
    wacc, w1s, w1r, w2s, w2r, w3s, w3r,
    a_sem, g_loc, g_s, g_r, b_s, b_r, st_sem, fa_s, fa_r, fw_s, fw_r, fb_s, fb_r,
    l_s, l_r, btc_sem, fin_sem, rx_s, rx_r, rx_l, rl_sem, ll_sem, lo_sem,
    w1_s, w1_q, w2_s, w2_q, w3_sem,
):
    chans, seqs, toks, nq, nl, quarter = dims
    n_depth, n_row, n_col = (lax.axis_size(x) for x in ("depth", "row", "col"))
    depth, row, col = (lax.axis_index(x) for x in ("depth", "row", "col"))
    core = lax.rem(depth, 2)
    buddy = depth + 1 - 2 * core
    pair = row + 1 - 2 * lax.rem(row, 2)
    far = 2 - 2 * (row // 2)
    inner = jnp.logical_or(row == 1, row == 2)
    jq = g_all.shape[0] // nq
    wide = jq * chans
    i_own = g_hbm.shape[2]
    lw = a_all.shape[1] // nl

    def remote(src, dst, ss, rs, **where):
        return pltpu.make_async_remote_copy(
            src_ref=src, dst_ref=dst, send_sem=ss, recv_sem=rs,
            device_id=where, device_id_type=MESH,
        )

    barrier = pltpu.get_barrier_semaphore()
    peers = [{"depth": lax.rem(depth + m, n_depth)} for m in range(1, n_depth)]
    peers += [{"row": lax.rem(row + m, n_row)} for m in range(1, n_row)]
    peers += [{"col": 1 - col}, {"depth": buddy, "col": 1 - col}]
    for where in peers:
        pl.semaphore_signal(barrier, inc=1, device_id=where, device_id_type=MESH)
    pl.semaphore_wait(barrier, len(peers))

    def g_copy(m, q):
        to = lax.rem(depth + m + 1, n_depth)
        js = pl.ds(pl.multiple_of(q * jq, jq), jq)
        rows = pl.ds(pl.multiple_of(depth * i_own, i_own), i_own)
        return remote(
            g_hbm.at[lax.rem(to, 2), js], g_all.at[js, rows], g_s.at[m, q], g_r.at[m, q], depth=to
        )

    def b_copy(q):
        rows = pl.ds(pl.multiple_of(q * wide, wide), wide)
        return remote(bt_hbm.at[1 - core, rows], btr.at[rows], b_s.at[q], b_r.at[q], depth=buddy)

    own_rows = pl.ds(pl.multiple_of(core * seqs, seqs), seqs)
    a_local = pltpu.make_async_copy(a_hbm, a_all.at[own_rows], a_sem.at[0])
    a_remote = remote(a_hbm, a_all.at[own_rows], a_sem.at[1], a_sem.at[2], depth=buddy)
    g_local = pltpu.make_async_copy(
        g_hbm.at[core], g_all.at[:, pl.ds(pl.multiple_of(depth * i_own, i_own), i_own)], g_loc.at[0]
    )
    for m in range(n_depth - 1):
        g_copy(m, 0).start()
    a_remote.start()
    g_local.start()
    a_local.start()

    for m in range(n_depth - 1):
        g_copy(m, 0).wait_send()
    for m in range(n_depth - 1):
        g_copy(m, 1).start()
    g_local.wait()

    def bt_load(q, slot):
        rows = pl.ds(pl.multiple_of(q * wide, wide), wide)
        return (
            pltpu.make_async_copy(bt_hbm.at[core, rows], btc.at[slot, core], btc_sem.at[slot, 0]),
            pltpu.make_async_copy(btr.at[rows], btc.at[slot, 1 - core], btc_sem.at[slot, 1]),
        )

    def build_b(q):
        for cp in bt_load(q, 0):
            cp.wait()
        cols = pl.ds(pl.multiple_of(q * wide, wide), wide)
        for h in range(2):
            b_all[h * seqs:(h + 1) * seqs, cols] = lax.dot_general(
                eye_ref[...], btc[0, h], (((1,), (1,)), ((), ())), preferred_element_type=F32
            ).astype(BF16)

    piece = 2 * quarter

    def target(t, count):
        return pl.ds(pl.multiple_of(t * piece, piece), count * piece)

    def fa_copy(q):
        return remote(
            rown.at[q, target(pair, 1)], rfa.at[q], fa_s.at[q], fa_r.at[q], row=pair
        )

    def fw_copy(q):
        return remote(
            rown.at[q, target(far, 2)], rfw.at[q], fw_s.at[q], fw_r.at[q], row=pair
        )

    def fb_copy(m, u):
        return remote(
            fsum.at[lax.rem(m, 2), u * piece:(u + 1) * piece], rfb.at[m], fb_s.at[u, m], fb_r.at[m], row=far + u
        )

    def fin_loads(m):
        return (
            pltpu.make_async_copy(rfw.at[m], fin.at[0], fin_sem.at[0]),
            pltpu.make_async_copy(rown.at[m, target(far, 2)], fin.at[1], fin_sem.at[1]),
        )

    def forward_start(m):
        fw_copy(m).wait_recv()
        for cp in fin_loads(m):
            cp.start()

    def forward_finish(m):
        for cp in fin_loads(m):
            cp.wait()

        @pl.when(m >= 2)
        def _():
            for u in range(2):
                fb_copy(m - 2, u).wait_send()

        fsum[lax.rem(m, 2)] = (fin[0].astype(F32) + fin[1].astype(F32)).astype(BF16)
        for u in range(2):
            fb_copy(m, u).start()

    def right_step(q, carry):
        turn = jnp.logical_and(inner, jnp.logical_and(q >= 3, lax.rem(q, 2) == 1))
        m_now = jnp.maximum((q - 3) // 2, 0)

        @pl.when(turn)
        def _():
            forward_start(m_now)

        @pl.when(q < nq - 2)
        def _():
            for m in range(n_depth - 1):
                g_copy(m, q + 2).start()

        for m in range(n_depth - 1):
            g_copy(m, q).wait_recv()
        b_copy(q).start()
        rows = pl.multiple_of(q * wide, wide)
        for u in range(jq // 2):
            pair_g = g_all[pl.ds(q * jq + 2 * u, 2)].reshape(2 * toks, -1)
            d = lax.dot_general(
                w_ref[...], pair_g, (((1,), (1,)), ((), ())), preferred_element_type=F32
            ).astype(BF16)
            for v in range(2):
                at = pl.multiple_of(rows + (2 * u + v) * chans, chans)
                for c in range(chans):
                    d_all[pl.ds(at, chans), c * toks:(c + 1) * toks] = d[
                        c * chans:(c + 1) * chans, v * toks:(v + 1) * toks
                    ]

        @pl.when(q == 0)
        def _():
            a_local.wait()
            a_remote.wait()

        half = wide // 2
        for n in range(2):
            at = pl.multiple_of(rows + n * half, half)
            r = lax.dot_general(
                a_all[...], d_all[pl.ds(at, half)], (((1,), (1,)), ((), ())), preferred_element_type=F32
            )
            r = (r * inv).astype(BF16)
            for h in range(2):
                for t in range(n_row):
                    first = h * seqs + t * quarter
                    at = t * piece + h * quarter
                    stage[0, at:at + quarter, n * half:(n + 1) * half] = r[first:first + quarter]
        out = pltpu.make_async_copy(stage.at[0], rown.at[q], st_sem.at[0])
        out.start()

        @pl.when(q > 0)
        def _():
            build_b(q - 1)

        b_copy(q).wait_recv()
        for cp in bt_load(q, 0):
            cp.start()
        out.wait()

        @pl.when(jnp.logical_not(inner))
        def _():
            fw_copy(q).start()

        @pl.when(inner)
        def _():
            fa_copy(q).start()

        @pl.when(turn)
        def _():
            forward_finish(m_now)

        return carry

    lax.fori_loop(0, nq, right_step, 0)
    build_b(nq - 1)

    def l_copy(l, r):
        kk = core if r == 1 else 1 - core
        tx = col if r == 0 else 1 - col
        where = ({"depth": buddy}, {"col": 1 - col}, {"depth": buddy, "col": 1 - col})[r]
        return remote(
            lown.at[l, target(kk * 2 + tx, 1)], lrecv.at[r, l], l_s.at[r, l], l_r.at[r, l], **where
        )

    def l_out(l):
        slot = lax.rem(l, 2)
        return pltpu.make_async_copy(stage.at[slot], lown.at[l], st_sem.at[slot])

    def l_send(l):
        l_out(l).wait()
        for r in (2, 1, 0):
            l_copy(l, r).start()

    def left_step(l, carry):
        turn = jnp.logical_and(inner, lax.rem(l, 3) == 1)
        m_now = 3 + l // 3

        @pl.when(turn)
        def _():
            forward_start(m_now)

        @pl.when(jnp.logical_not(inner))
        def _():
            fa_copy(l).start()

        half = lw // 2
        slot = lax.rem(l, 2)
        for n in range(2):
            cols = pl.ds(pl.multiple_of(l * lw + n * half, half), half)
            x = jnp.dot(b_all[...], d_all[:, cols], preferred_element_type=F32)
            x = (x * inv).astype(BF16)
            stage[slot, :, n * half:(n + 1) * half] = x
        l_out(l).start()

        @pl.when(l > 0)
        def _():
            l_send(l - 1)

        @pl.when(turn)
        def _():
            forward_finish(m_now)

        return carry

    for cp in bt_load(0, 0):
        cp.start()
    lax.fori_loop(0, nl, left_step, 0)
    l_send(nl - 1)

    wacc[...] = jnp.zeros_like(wacc)

    def right_loads(m):
        srcs = (rown.at[m, target(row, 1)], rfa.at[m], rfb.at[m])
        return [
            pltpu.make_async_copy(
                src, b_all.at[n * piece:(n + 1) * piece, 7 * wide:8 * wide], rl_sem.at[n]
            )
            for n, src in enumerate(srcs)
        ]

    def right_out(m, sent=False):
        slot = lax.rem(m, 2)
        cols = pl.ds(pl.multiple_of((core * nq + m) * wide, wide), wide)

        def rows(k):
            at = slot * piece + k * quarter
            return b_all.at[pl.ds(pl.multiple_of(at, quarter), quarter), 6 * wide:7 * wide]

        away = remote(rows(1 - core), rfin.at[:, cols], rx_s.at[m], rx_r.at[m], depth=buddy)
        if sent:
            return away
        return pltpu.make_async_copy(rows(core), rfin.at[:, cols], rx_l.at[m]), away

    def right_final_start(m):
        fa_copy(m).wait_recv()
        fb_copy(m, 0).wait_recv()
        for cp in right_loads(m):
            cp.start()

    def right_final_finish(m):
        for cp in right_loads(m):
            cp.wait()

        @pl.when(m >= 2)
        def _():
            mine, theirs = right_out(m - 2)
            mine.wait()
            theirs.wait_send()

        total = sum(
            b_all[n * piece:(n + 1) * piece, 7 * wide:8 * wide].astype(F32) for n in range(3)
        ).astype(BF16)
        at = pl.multiple_of(lax.rem(m, 2) * piece, piece)
        b_all[pl.ds(at, piece), 6 * wide:7 * wide] = total
        for cp in right_out(m):
            cp.start()

    def left_loads(p):
        cps = []
        for h in range(2):
            l = 2 * p + h
            srcs = [lown.at[l, target(core * 2 + col, 1)]] + [lrecv.at[r, l] for r in range(3)]
            for n, src in enumerate(srcs):
                dst = b_all.at[n * piece:(n + 1) * piece, h * lw:(h + 1) * lw]
                cps.append(pltpu.make_async_copy(src, dst, ll_sem.at[h, n]))
        return cps

    def left_out_copy(p):
        cs = pl.ds(pl.multiple_of(p * 8, 8), 8)
        return pltpu.make_async_copy(lbuf.reshape(piece, 8, toks), left_out.at[:, cs], lo_sem.at[0])

    def left_final_start(p):
        for h in range(2):
            for r in range(3):
                l_copy(2 * p + h, r).wait_recv()
        for cp in left_loads(p):
            cp.start()

    def left_final_finish(p):
        for cp in left_loads(p):
            cp.wait()

        @pl.when(p >= 1)
        def _():
            left_out_copy(p - 1).wait()

        for h in range(2):
            for c in range(4):
                cols = slice(h * lw + c * toks, h * lw + (c + 1) * toks)
                lbuf[pl.ds(4 * h + c, piece, stride=8), :] = sum(
                    b_all[n * piece:(n + 1) * piece, cols].astype(F32) for n in range(4)
                )
        left_out_copy(p).start()

    def outer_step(o, carry):
        left_turn = o >= nq - 3
        turn = jnp.logical_and(inner, jnp.logical_or(o == 1, o == 3))
        m_now = 6 + o // 3
        p_now = jnp.maximum(o - (nq - 3), 0)

        @pl.when(turn)
        def _():
            forward_start(m_now)

        @pl.when(o < early)
        def _():
            right_final_start(o)

        @pl.when(left_turn)
        def _():
            left_final_start(p_now)

        slot = lax.rem(o, 2)
        for cp in bt_load(o, slot):
            cp.wait()

        @pl.when(o < nq - 1)
        def _():
            for cp in bt_load(o + 1, 1 - slot):
                cp.start()

        width = 512
        for n in range(a_all.shape[1] // width):
            cols = slice(n * width, (n + 1) * width)
            x = jnp.dot(btc[slot, 0], a_all[:seqs, cols], preferred_element_type=F32)
            x += jnp.dot(btc[slot, 1], a_all[seqs:, cols], preferred_element_type=F32)
            d_all[:wide, cols] = (x * inv).astype(BF16)
        right = g_all[pl.ds(pl.multiple_of(o * jq, jq), jq)].reshape(jq * toks, -1)
        cg = 8
        for c0 in range(0, chans, cg):
            left = jnp.concatenate(
                [
                    jnp.concatenate(
                        [
                            d_all[j * chans:(j + 1) * chans, c * toks:(c + 1) * toks]
                            for j in range(jq)
                        ],
                        axis=1,
                    )
                    for c in range(c0, c0 + cg)
                ],
                axis=0,
            )
            wacc[c0 * chans:(c0 + cg) * chans] += jnp.dot(left, right, preferred_element_type=F32)

        @pl.when(turn)
        def _():
            forward_finish(m_now)

        @pl.when(o < early)
        def _():
            right_final_finish(o)

        @pl.when(left_turn)
        def _():
            left_final_finish(p_now)

        return carry

    early = nq - 1
    lax.fori_loop(0, nq, outer_step, 0)

    n1 = wacc.shape[0] // n_depth
    n2 = n1 // n_row
    n3 = n2 // 2

    def part(ref, index, size):
        return ref.at[pl.ds(pl.multiple_of(index * size, size), size)]

    def w1_copy(m):
        to = lax.rem(depth + m + 1, n_depth)
        return remote(part(w1s, to, n1), w1r.at[m], w1_s.at[m], w1_q.at[m], depth=to)

    def w2_copy(m):
        to = lax.rem(row + m + 1, n_row)
        return remote(part(w2s, to, n2), w2r.at[m], w2_s.at[m], w2_q.at[m], row=to)

    w3_copy = remote(part(w3s, 1 - col, n3), w3r, w3_sem.at[0], w3_sem.at[1], col=1 - col)

    w1s[...] = wacc[...].astype(BF16)
    for m in range(n_depth - 1):
        w1_copy(m).start()
    left_final_start(nl // 2 - 1)
    left_final_finish(nl // 2 - 1)
    for m in range(n_depth - 1):
        w1_copy(m).wait()
    w2s[...] = part(wacc, depth, n1)[...] + sum(w1r[m].astype(F32) for m in range(n_depth - 1))
    for m in range(n_row - 1):
        w2_copy(m).start()
    right_final_start(nq - 1)
    right_final_finish(nq - 1)
    for m in range(n_row - 1):
        w2_copy(m).wait()
    w3s[...] = part(w2s, row, n2)[...] + sum(w2r[m] for m in range(n_row - 1))
    w3_copy.start()

    @pl.when(inner)
    def _():
        for m in (nq - 2, nq - 1):
            for u in range(2):
                fb_copy(m, u).wait_send()

    for m in (nq - 2, nq - 1):
        mine, theirs = right_out(m)
        mine.wait()
        theirs.wait_send()
    left_out_copy(nl // 2 - 1).wait()

    def drain(q, carry):
        @pl.when(q > 0)
        def _():
            for m in range(n_depth - 1):
                g_copy(m, q).wait_send()

        b_copy(q).wait_send()
        fa_copy(q).wait_send()
        right_out(q, True).wait_recv()

        @pl.when(jnp.logical_not(inner))
        def _():
            fw_copy(q).wait_send()

        return carry

    lax.fori_loop(0, nq, drain, 0)

    def drain_l(l, carry):
        for r in range(3):
            l_copy(l, r).wait_send()
        return carry

    lax.fori_loop(0, nl, drain_l, 0)
    w3_copy.wait()
    w_out[...] = part(w3s, col, n3)[...] + w3r[...]


def mega_call(a2, bt, gt, w, inv, chans, toks):
    seqs, ci = a2.shape
    jh, je = gt.shape[1], bt.shape[1]
    i_own, pair_ch = gt.shape[2:]
    n_depth, n_row = lax.axis_size("depth"), lax.axis_size("row")
    nq = nl = 8
    wide = je // nq
    lw = ci // nl
    quarter = seqs // n_row
    piece = 2 * quarter
    n1 = chans * chans // n_depth
    n2 = n1 // n_row
    n3 = n2 // 2
    hbm = lambda *s: jax.ShapeDtypeStruct(s, BF16)
    dma = lambda *s: pltpu.SemaphoreType.DMA(s)
    anyspec = pl.BlockSpec(memory_space=pl.ANY)
    vmem = pl.BlockSpec(memory_space=pltpu.VMEM)
    eye = jnp.eye(seqs, dtype=BF16)
    return pl.pallas_call(
        functools.partial(mega_kernel, (chans, seqs, toks, nq, nl, quarter), inv),
        out_shape=(
            hbm(nq, n_row * piece, wide),
            hbm(nq, 2 * piece, wide),
            hbm(nq, piece, wide),
            hbm(nq, piece, wide),
            hbm(nl, n_row * piece, lw),
            hbm(3, nl, piece, lw),
            hbm(je, seqs),
            hbm(quarter, 2 * je),
            jax.ShapeDtypeStruct((piece, chans, toks), F32),
            jax.ShapeDtypeStruct((n3, pair_ch), F32),
        ),
        in_specs=[anyspec, anyspec, anyspec, vmem, vmem],
        out_specs=(anyspec,) * 9 + (vmem,),
        scratch_shapes=[
            pltpu.VMEM((2 * seqs, ci), BF16),
            pltpu.VMEM((je, ci), BF16),
            pltpu.VMEM((2 * seqs, je), BF16),
            pltpu.VMEM((jh, i_own * n_depth, pair_ch), BF16),
            pltpu.VMEM((2, n_row * piece, wide), BF16),
            pltpu.VMEM((2, 2, wide, seqs), BF16),
            pltpu.VMEM((2, 2 * piece, wide), BF16),
            pltpu.VMEM((2, 2 * piece, wide), BF16),
            pltpu.VMEM((piece * 8, toks), F32),
            pltpu.VMEM((chans * chans, pair_ch), F32),
            pltpu.VMEM((chans * chans, pair_ch), BF16),
            pltpu.VMEM((n_depth - 1, n1, pair_ch), BF16),
            pltpu.VMEM((n1, pair_ch), F32),
            pltpu.VMEM((n_row - 1, n2, pair_ch), F32),
            pltpu.VMEM((n2, pair_ch), F32),
            pltpu.VMEM((n3, pair_ch), F32),
            dma(3), dma(1), dma(n_depth - 1, nq), dma(n_depth - 1, nq), dma(nq), dma(nq), dma(2),
            dma(nq), dma(nq), dma(nq), dma(nq), dma(2, nq), dma(nq),
            dma(3, nl), dma(3, nl), dma(2, 2), dma(2),
            dma(nq), dma(nq), dma(nq), dma(3), dma(2, 4), dma(1),
            dma(n_depth - 1), dma(n_depth - 1), dma(n_row - 1), dma(n_row - 1), dma(2),
        ],
        compiler_params=pltpu.CompilerParams(
            vmem_limit_bytes=MEGA_VMEM, collective_id=0, has_side_effects=True
        ),
        cost_estimate=cost(6 * seqs * 2 * je * ci, 8 * seqs * ci),
        name="mega",
    )(a2, bt, gt, w, eye)


def post_kernel(chans, l_ref, r_ref, eye_ref, l_out, r_out, tmp, mix):
    rows, je = r_ref.shape
    wide = eye_ref.shape[0]
    group, toks = r_out.shape[1:]
    l_out[...] = l_ref[...]

    @pl.when(pl.program_id(0) == 0)
    def _():
        for n in range(je // wide):
            tmp[n * wide:(n + 1) * wide, :rows] = lax.dot_general(
                eye_ref[...], r_ref[:, n * wide:(n + 1) * wide], (((1,), (1,)), ((), ())),
                preferred_element_type=F32,
            )

    first = pl.program_id(0) * group
    lanes = mix.shape[2]
    for e in range(group):
        x = tmp[pl.ds(first + e, toks, stride=chans), :][:, :rows].astype(BF16)
        y = lax.dot_general(
            eye_ref[:rows, :rows], x, (((1,), (1,)), ((), ())), preferred_element_type=F32
        )
        for k in range(mix.shape[0]):
            mix[k, pl.ds(e, rows, stride=group), :] = y[:, k * lanes:(k + 1) * lanes]
    for k in range(mix.shape[0]):
        r_out[:, :, k * lanes:(k + 1) * lanes] = mix[k].reshape(rows, group, lanes)


def post_call(left, rfin, toks):
    srows, chans, width = left.shape
    rows, je = rfin.shape
    steps = chans // 8
    return pl.pallas_call(
        functools.partial(post_kernel, chans),
        out_shape=(
            jax.ShapeDtypeStruct(left.shape, F32),
            jax.ShapeDtypeStruct((rows, chans, toks), F32),
        ),
        grid=(steps,),
        in_specs=[
            pl.BlockSpec((srows // steps, chans, width), lambda n: (n, 0, 0)),
            pl.BlockSpec((rows, je), lambda n: (0, 0)),
            pl.BlockSpec((256, 256), lambda n: (0, 0)),
        ],
        out_specs=(
            pl.BlockSpec((srows // steps, chans, width), lambda n: (n, 0, 0)),
            pl.BlockSpec((rows, 8, toks), lambda n: (0, n, 0)),
        ),
        scratch_shapes=[pltpu.VMEM((je, 128), F32), pltpu.VMEM((toks // 128, rows * 8, 128), F32)],
        compiler_params=params(),
        name="post",
    )(left, rfin, jnp.eye(256, dtype=BF16))


def mega_body(left_factor, right_factor, out_weight, pair_cotangent):
    seqs, chans, rows = left_factor.shape
    toks = right_factor.shape[2]
    inv = 1.0 / (seqs * lax.axis_size("depth"))
    jh = toks // 2
    a2 = left_factor.reshape(seqs, chans * rows)
    bt = jnp.transpose(right_factor, (2, 1, 0)).reshape(2, jh * chans, seqs)
    gt = jnp.transpose(pair_cotangent, (1, 0, 2)).reshape(2, jh, -1, pair_cotangent.shape[2])
    *_, rfin, left_grad, weight_grad = mega_call(a2, bt, gt, out_weight, inv, chans, rows)

    left_grad, right_grad = post_call(left_grad, rfin, toks)
    return left_grad, right_grad, weight_grad


def plain_body(left_factor, right_factor, out_weight, pair_cotangent):
    seq_total = left_factor.shape[0] * lax.axis_size("depth")
    chans = left_factor.shape[1]
    rows_here = left_factor.shape[2]
    cols_here = right_factor.shape[2]
    width = out_weight.shape[0]
    pair_ch = out_weight.shape[1]
    natural = jnp.einsum("sci,sej->ciej", left_factor, right_factor, preferred_element_type=F32) / seq_total
    outer = jnp.transpose(natural.astype(BF16), (1, 3, 0, 2)).reshape(rows_here * cols_here, width)
    piece = lax.all_gather(pair_cotangent, "depth", axis=0, tiled=True)
    grad_two = piece.reshape(rows_here * cols_here, pair_ch)
    delta = jnp.dot(grad_two, out_weight.T, preferred_element_type=F32).astype(BF16)
    weight_acc = jnp.dot(outer.T, grad_two, preferred_element_type=F32)
    delta_four = delta.reshape(rows_here, cols_here, chans, chans)
    left_part = jnp.einsum("ijce,sej->sci", delta_four, right_factor, preferred_element_type=F32) / seq_total
    right_part = jnp.einsum("ijce,sci->sej", delta_four, left_factor, preferred_element_type=F32) / seq_total
    left_grad = lax.psum_scatter(left_part, "col", scatter_dimension=0, tiled=True)
    right_grad = lax.psum_scatter(right_part, "row", scatter_dimension=0, tiled=True)
    middle = lax.psum_scatter(weight_acc, ("depth", "row"), scatter_dimension=0, tiled=True)
    weight_grad = lax.psum_scatter(middle, "col", scatter_dimension=0, tiled=True)
    return left_grad, right_grad, weight_grad


def body(left_factor, right_factor, out_weight, pair_cotangent):
    seqs, chans, rows = left_factor.shape
    toks = right_factor.shape[2]
    fits = toks % 128 == 0 and toks <= 256 and rows % 32 == 0 and chans == 32 and seqs <= 512
    shape = tuple(lax.axis_size(x) for x in ("depth", "row", "col"))
    mega = (
        fits and shape == (4, 4, 2) and toks == 256 and rows == 128 and seqs % 64 == 0
        and out_weight.shape[1] == 128
    )
    run = mega_body if mega else fused_body if fits else plain_body
    return run(left_factor, right_factor, out_weight, pair_cotangent)


def solution(mesh):
    return jax.shard_map(
        body,
        mesh=mesh,
        in_specs=(
            P("depth", None, "row"),
            P("depth", None, "col"),
            P(),
            P(("row", "depth"), "col", None),
        ),
        out_specs=(
            P(("depth", "col"), None, "row"),
            P(("depth", "row"), None, "col"),
            P(("depth", "row", "col"), None),
        ),
        check_vma=False,
    )
```

```python
import functools

import jax
import jax.numpy as jnp
import numpy as np
from jax import lax
from jax.experimental import pallas as pl
from jax.experimental.pallas import tpu as pltpu
from jax.sharding import PartitionSpec as P

F32 = jnp.float32
BF16 = jnp.bfloat16
VMEM_CAP = 60 * 1024 * 1024
MEGA_VMEM = 62 * 1024 * 1024
MESH = pl.DeviceIdType.MESH


def params():
    return pltpu.CompilerParams(vmem_limit_bytes=VMEM_CAP)


def cost(flops, nbytes):
    return pl.CostEstimate(flops=flops, bytes_accessed=nbytes, transcendentals=0)


def outer_kernel(inv, at_ref, b_ref, o_ref):
    width = 512 if o_ref.shape[1] % 512 == 0 else o_ref.shape[1]
    for n in range(o_ref.shape[1] // width):
        cols = slice(n * width, (n + 1) * width)
        acc = jnp.dot(at_ref[...], b_ref[:, cols], preferred_element_type=F32)
        o_ref[:, cols] = (acc * inv).astype(BF16)


def outer_call(at, b2, inv, tm, tn, part, cols):
    rows, seqs = at.shape
    first = part * cols // tn
    return pl.pallas_call(
        functools.partial(outer_kernel, inv),
        out_shape=jax.ShapeDtypeStruct((rows, cols), BF16),
        grid=(cols // tn, rows // tm),
        in_specs=[
            pl.BlockSpec((tm, seqs), lambda n, m: (m, 0)),
            pl.BlockSpec((seqs, tn), lambda n, m: (0, n + first)),
        ],
        out_specs=pl.BlockSpec((tm, tn), lambda n, m: (m, n)),
        compiler_params=params(),
        cost_estimate=cost(2 * rows * cols * seqs, 2 * rows * cols + 2 * seqs * (rows + cols)),
        name=f"outer_{part}",
    )(at, b2)


def delta_kernel(inv, chans, toks, w_ref, g_ref, a_ref, d_ref, r_ref, acc_ref):
    step = pl.program_id(0)
    here = g_ref.shape[0]
    eb = w_ref.shape[0] // chans

    def one(i, carry):
        d = lax.dot_general(
            w_ref[...], g_ref[i], (((1,), (1,)), ((), ())), preferred_element_type=F32
        ).astype(BF16)
        at = pl.multiple_of(i * chans, chans)
        for e in range(eb):
            d_ref[pl.ds(at, chans), e * toks:(e + 1) * toks] = d[e * chans:(e + 1) * chans]
        return carry

    lax.fori_loop(0, here, one, 0, unroll=8)

    @pl.when(step == 0)
    def _():
        acc_ref[...] = jnp.zeros_like(acc_ref)

    for e in range(eb):
        cols = slice(e * toks, (e + 1) * toks)
        acc_ref[:, cols] += jnp.dot(a_ref[...], d_ref[:, cols], preferred_element_type=F32)

    @pl.when(step == pl.num_programs(0) - 1)
    def _():
        r_ref[...] = (acc_ref[...] * inv).astype(BF16)


def delta_call(w_ec, g, a2, inv, chans, part, eb, ti):
    rows, toks, pair_ch = g.shape
    seqs = a2.shape[0]
    wide = eb * toks
    return pl.pallas_call(
        functools.partial(delta_kernel, inv, chans, toks),
        out_shape=(
            jax.ShapeDtypeStruct((rows * chans, wide), BF16),
            jax.ShapeDtypeStruct((seqs, wide), BF16),
        ),
        grid=(rows // ti,),
        in_specs=[
            pl.BlockSpec((eb * chans, pair_ch), lambda m: (part, 0)),
            pl.BlockSpec((ti, toks, pair_ch), lambda m: (m, 0, 0)),
            pl.BlockSpec((seqs, ti * chans), lambda m: (0, m)),
        ],
        out_specs=(
            pl.BlockSpec((ti * chans, wide), lambda m: (m, 0)),
            pl.BlockSpec((seqs, wide), lambda m: (0, 0)),
        ),
        scratch_shapes=[pltpu.VMEM((seqs, wide), F32)],
        compiler_params=params(),
        cost_estimate=cost(
            2 * rows * chans * wide * (seqs + 2 * pair_ch),
            2 * rows * (chans * wide + toks * pair_ch + chans * seqs),
        ),
        name=f"delta_right_{part}",
    )(w_ec, g, a2)


def left_kernel(inv, parts, b_ref, *refs):
    d_refs, o_ref = refs[:parts], refs[parts]
    wide = d_refs[0].shape[1]
    acc = None
    for k in range(parts):
        term = lax.dot_general(
            b_ref[:, k * wide:(k + 1) * wide],
            d_refs[k][...],
            (((1,), (1,)), ((), ())),
            preferred_element_type=F32,
        )
        acc = term if acc is None else acc + term
    o_ref[...] = (acc * inv).astype(BF16)


def left_call(b2, ds, inv, tn):
    seqs = b2.shape[0]
    rows, wide = ds[0].shape
    parts = len(ds)
    return pl.pallas_call(
        functools.partial(left_kernel, inv, parts),
        out_shape=jax.ShapeDtypeStruct((seqs, rows), BF16),
        grid=(rows // tn,),
        in_specs=[pl.BlockSpec((seqs, parts * wide), lambda m: (0, 0))]
        + [pl.BlockSpec((tn, wide), lambda m: (m, 0))] * parts,
        out_specs=pl.BlockSpec((seqs, tn), lambda m: (0, m)),
        compiler_params=params(),
        cost_estimate=cost(2 * seqs * rows * wide * parts, 2 * rows * wide * parts + 4 * seqs * rows),
        name="left",
    )(b2, *ds)


def weight_kernel(chans, *refs):
    o_refs, g_ref, w_ref = refs[:-2], refs[-2], refs[-1]
    ti, toks, pair_ch = g_ref.shape
    per = o_refs[0].shape[1] // toks

    @pl.when(pl.program_id(0) == 0)
    def _():
        w_ref[...] = jnp.zeros_like(w_ref)

    group = 4
    eg = 8 if per % 8 == 0 else 1

    def one(k, carry):
        first = pl.multiple_of(k * group, group)
        right = g_ref[pl.ds(first, group)].reshape(group * toks, pair_ch)
        for h, o_ref in enumerate(o_refs):
            for e0 in range(0, per, eg):
                left = jnp.concatenate(
                    [
                        jnp.concatenate(
                            [
                                o_ref[
                                    pl.ds(pl.multiple_of((first + i) * chans, chans), chans),
                                    e * toks:(e + 1) * toks,
                                ]
                                for i in range(group)
                            ],
                            axis=1,
                        )
                        for e in range(e0, e0 + eg)
                    ],
                    axis=0,
                )
                at = (h * per + e0) * chans
                w_ref[at:at + eg * chans] += jnp.dot(left, right, preferred_element_type=F32)
        return carry

    lax.fori_loop(0, ti // group, one, 0)


def weight_call(outers, g, chans, ti):
    rows, toks, pair_ch = g.shape
    cols = outers[0].shape[1]
    width = cols * len(outers) // toks * chans
    return pl.pallas_call(
        functools.partial(weight_kernel, chans),
        out_shape=jax.ShapeDtypeStruct((width, pair_ch), F32),
        grid=(rows // ti,),
        in_specs=[pl.BlockSpec((ti * chans, cols), lambda m: (m, 0))] * len(outers)
        + [pl.BlockSpec((ti, toks, pair_ch), lambda m: (m, 0, 0))],
        out_specs=pl.BlockSpec((width, pair_ch), lambda m: (0, 0)),
        compiler_params=params(),
        cost_estimate=cost(4 * rows * toks * width * pair_ch, 2 * rows * toks * width),
        name="weight",
    )(*outers, g)


def fused_body(left_factor, right_factor, out_weight, pair_cotangent):
    seqs, chans, rows = left_factor.shape
    toks = right_factor.shape[2]
    pair_ch = out_weight.shape[1]
    inv = 1.0 / (seqs * lax.axis_size("depth"))
    n_col = lax.axis_size("col")
    parts = 4
    eb = chans // parts

    g = lax.all_gather(pair_cotangent, "depth", axis=0, tiled=True)
    a2 = jnp.transpose(left_factor, (0, 2, 1)).reshape(seqs, rows * chans)
    at = jnp.transpose(left_factor, (2, 1, 0)).reshape(rows * chans, seqs)
    b2 = right_factor.reshape(seqs, chans * toks)
    w_ec = jnp.transpose(out_weight.reshape(chans, chans, pair_ch), (1, 0, 2)).reshape(
        chans * chans, pair_ch
    )

    half_cols = b2.shape[1] // 2
    outer_a = outer_call(at, b2, inv, 16 * chans, eb * toks, 0, half_cols)
    g, outer_a = lax.optimization_barrier((g, outer_a))

    ds, rights = [], []
    for k in range(parts):
        d, r = delta_call(w_ec, g, a2, inv, chans, k, eb, 32)
        ds.append(d)
        r, g = lax.optimization_barrier((r, g))
        rights.append(lax.psum_scatter(r, "row", scatter_dimension=0, tiled=True))
    left = left_call(b2, ds, inv, 8 * chans)
    left, at, b2 = lax.optimization_barrier((left, at, b2))
    if n_col == 2:
        half = seqs // 2
        me = lax.axis_index("col")
        mine = lax.dynamic_slice_in_dim(left, me * half, half, 0)
        theirs = lax.dynamic_slice_in_dim(left, (1 - me) * half, half, 0)
        theirs, at, b2 = lax.optimization_barrier((theirs, at, b2))
        got = lax.ppermute(theirs, "col", [(0, 1), (1, 0)])
        left_grad = mine.astype(F32) + got.astype(F32)
    else:
        left_grad = lax.psum_scatter(left, "col", scatter_dimension=0, tiled=True).astype(F32)
    left_grad = jnp.transpose(left_grad.reshape(-1, rows, chans), (0, 2, 1))
    outer_b = outer_call(at, b2, inv, 16 * chans, eb * toks, 1, half_cols)
    weight_acc = weight_call((outer_a, outer_b), g, chans, 8)
    weight_acc = jnp.transpose(weight_acc.reshape(chans, chans, pair_ch), (1, 0, 2)).reshape(
        chans * chans, pair_ch
    )
    axes = ("depth", "row", "col")
    count = lax.axis_size(axes)
    pieces = weight_acc.reshape(count, chans * chans // count, pair_ch)
    pieces = lax.all_to_all(pieces, axes, split_axis=0, concat_axis=0, tiled=True)
    rights = [r.reshape(-1, eb, toks) for r in rights]
    right_grad = jnp.concatenate(rights, axis=1).astype(F32)
    pieces, left_grad, right_grad = lax.optimization_barrier((pieces, left_grad, right_grad))
    weight_grad = jnp.sum(pieces, axis=0)
    return left_grad, right_grad, weight_grad


def mega_kernel(
    dims, inv, a_hbm, bt_hbm, g_hbm, w_ref, eye_ref,
    rown, rfw, rfa, rfb, lown, lrecv, btr, rfin, left_out, w_out,
    a_all, d_all, b_all, g_all, stage, btc, fin, fsum, lbuf,
    wacc, w1s, w1r, w2s, w2r, w3s, w3r,
    a_sem, g_loc, g_s, g_r, b_s, b_r, st_sem, fa_s, fa_r, fw_s, fw_r, fb_s, fb_r,
    l_s, l_r, btc_sem, fin_sem, rx_s, rx_r, rx_l, rl_sem, ll_sem, lo_sem,
    w1_s, w1_q, w2_s, w2_q, w3_sem,
):
    chans, seqs, toks, nq, nl, quarter = dims
    n_depth, n_row, n_col = (lax.axis_size(x) for x in ("depth", "row", "col"))
    depth, row, col = (lax.axis_index(x) for x in ("depth", "row", "col"))
    core = lax.rem(depth, 2)
    buddy = depth + 1 - 2 * core
    pair = row + 1 - 2 * lax.rem(row, 2)
    far = 2 - 2 * (row // 2)
    inner = jnp.logical_or(row == 1, row == 2)
    jq = g_all.shape[0] // nq
    wide = jq * chans
    i_own = g_hbm.shape[2]
    lw = a_all.shape[1] // nl

    def remote(src, dst, ss, rs, **where):
        return pltpu.make_async_remote_copy(
            src_ref=src, dst_ref=dst, send_sem=ss, recv_sem=rs,
            device_id=where, device_id_type=MESH,
        )

    barrier = pltpu.get_barrier_semaphore()
    peers = [{"depth": lax.rem(depth + m, n_depth)} for m in range(1, n_depth)]
    peers += [{"row": lax.rem(row + m, n_row)} for m in range(1, n_row)]
    peers += [{"col": 1 - col}, {"depth": buddy, "col": 1 - col}]
    for where in peers:
        pl.semaphore_signal(barrier, inc=1, device_id=where, device_id_type=MESH)
    pl.semaphore_wait(barrier, len(peers))

    def g_copy(m, q):
        to = lax.rem(depth + m + 1, n_depth)
        js = pl.ds(pl.multiple_of(q * jq, jq), jq)
        rows = pl.ds(pl.multiple_of(depth * i_own, i_own), i_own)
        return remote(
            g_hbm.at[lax.rem(to, 2), js], g_all.at[js, rows], g_s.at[m, q], g_r.at[m, q], depth=to
        )

    def b_copy(q):
        rows = pl.ds(pl.multiple_of(q * wide, wide), wide)
        return remote(bt_hbm.at[1 - core, rows], btr.at[rows], b_s.at[q], b_r.at[q], depth=buddy)

    own_rows = pl.ds(pl.multiple_of(core * seqs, seqs), seqs)
    a_local = pltpu.make_async_copy(a_hbm, a_all.at[own_rows], a_sem.at[0])
    a_remote = remote(a_hbm, a_all.at[own_rows], a_sem.at[1], a_sem.at[2], depth=buddy)
    g_local = pltpu.make_async_copy(
        g_hbm.at[core], g_all.at[:, pl.ds(pl.multiple_of(depth * i_own, i_own), i_own)], g_loc.at[0]
    )
    for m in range(n_depth - 1):
        g_copy(m, 0).start()
    a_remote.start()
    g_local.start()
    a_local.start()

    for m in range(n_depth - 1):
        g_copy(m, 0).wait_send()
    for m in range(n_depth - 1):
        g_copy(m, 1).start()
    g_local.wait()

    def bt_load(q, slot):
        rows = pl.ds(pl.multiple_of(q * wide, wide), wide)
        return (
            pltpu.make_async_copy(bt_hbm.at[core, rows], btc.at[slot, core], btc_sem.at[slot, 0]),
            pltpu.make_async_copy(btr.at[rows], btc.at[slot, 1 - core], btc_sem.at[slot, 1]),
        )

    def build_b(q):
        for cp in bt_load(q, 0):
            cp.wait()
        cols = pl.ds(pl.multiple_of(q * wide, wide), wide)
        for h in range(2):
            b_all[h * seqs:(h + 1) * seqs, cols] = lax.dot_general(
                eye_ref[...], btc[0, h], (((1,), (1,)), ((), ())), preferred_element_type=F32
            ).astype(BF16)

    piece = 2 * quarter

    def target(t, count):
        return pl.ds(pl.multiple_of(t * piece, piece), count * piece)

    def fa_copy(q):
        return remote(
            rown.at[q, target(pair, 1)], rfa.at[q], fa_s.at[q], fa_r.at[q], row=pair
        )

    def fw_copy(q):
        return remote(
            rown.at[q, target(far, 2)], rfw.at[q], fw_s.at[q], fw_r.at[q], row=pair
        )

    def fb_copy(m, u):
        return remote(
            fsum.at[lax.rem(m, 2), u * piece:(u + 1) * piece], rfb.at[m], fb_s.at[u, m], fb_r.at[m], row=far + u
        )

    def fin_loads(m):
        return (
            pltpu.make_async_copy(rfw.at[m], fin.at[0], fin_sem.at[0]),
            pltpu.make_async_copy(rown.at[m, target(far, 2)], fin.at[1], fin_sem.at[1]),
        )

    def forward_start(m):
        fw_copy(m).wait_recv()
        for cp in fin_loads(m):
            cp.start()

    def forward_finish(m):
        for cp in fin_loads(m):
            cp.wait()

        @pl.when(m >= 2)
        def _():
            for u in range(2):
                fb_copy(m - 2, u).wait_send()

        fsum[lax.rem(m, 2)] = (fin[0].astype(F32) + fin[1].astype(F32)).astype(BF16)
        for u in range(2):
            fb_copy(m, u).start()

    def right_step(q, carry):
        turn = jnp.logical_and(inner, jnp.logical_and(q >= 3, lax.rem(q, 2) == 1))
        m_now = jnp.maximum((q - 3) // 2, 0)

        @pl.when(turn)
        def _():
            forward_start(m_now)

        @pl.when(q < nq - 2)
        def _():
            for m in range(n_depth - 1):
                g_copy(m, q + 2).start()

        for m in range(n_depth - 1):
            g_copy(m, q).wait_recv()
        b_copy(q).start()
        rows = pl.multiple_of(q * wide, wide)
        for u in range(jq // 2):
            pair_g = g_all[pl.ds(q * jq + 2 * u, 2)].reshape(2 * toks, -1)
            d = lax.dot_general(
                w_ref[...], pair_g, (((1,), (1,)), ((), ())), preferred_element_type=F32
            ).astype(BF16)
            for v in range(2):
                at = pl.multiple_of(rows + (2 * u + v) * chans, chans)
                for c in range(chans):
                    d_all[pl.ds(at, chans), c * toks:(c + 1) * toks] = d[
                        c * chans:(c + 1) * chans, v * toks:(v + 1) * toks
                    ]

        @pl.when(q == 0)
        def _():
            a_local.wait()
            a_remote.wait()

        half = wide // 2
        for n in range(2):
            at = pl.multiple_of(rows + n * half, half)
            r = lax.dot_general(
                a_all[...], d_all[pl.ds(at, half)], (((1,), (1,)), ((), ())), preferred_element_type=F32
            )
            r = (r * inv).astype(BF16)
            for h in range(2):
                for t in range(n_row):
                    first = h * seqs + t * quarter
                    at = t * piece + h * quarter
                    stage[0, at:at + quarter, n * half:(n + 1) * half] = r[first:first + quarter]
        out = pltpu.make_async_copy(stage.at[0], rown.at[q], st_sem.at[0])
        out.start()

        @pl.when(q > 0)
        def _():
            build_b(q - 1)

        b_copy(q).wait_recv()
        for cp in bt_load(q, 0):
            cp.start()
        out.wait()

        @pl.when(jnp.logical_not(inner))
        def _():
            fw_copy(q).start()

        @pl.when(inner)
        def _():
            fa_copy(q).start()

        @pl.when(turn)
        def _():
            forward_finish(m_now)

        return carry

    lax.fori_loop(0, nq, right_step, 0)
    build_b(nq - 1)

    def l_copy(l, r):
        kk = core if r == 1 else 1 - core
        tx = col if r == 0 else 1 - col
        where = ({"depth": buddy}, {"col": 1 - col}, {"depth": buddy, "col": 1 - col})[r]
        return remote(
            lown.at[l, target(kk * 2 + tx, 1)], lrecv.at[r, l], l_s.at[r, l], l_r.at[r, l], **where
        )

    def l_out(l):
        slot = lax.rem(l, 2)
        return pltpu.make_async_copy(stage.at[slot], lown.at[l], st_sem.at[slot])

    def l_send(l):
        l_out(l).wait()
        for r in (2, 1, 0):
            l_copy(l, r).start()

    def direct_late(step):
        late = jnp.logical_and(step >= 5, step < nq + 5)

        @pl.when(jnp.logical_and(jnp.logical_not(inner), late))
        def _():
            fa_copy(step - 5).start()

    def left_step(l, carry):
        turn = jnp.logical_and(inner, lax.rem(l, 3) == 1)
        m_now = 3 + l // 3

        @pl.when(turn)
        def _():
            forward_start(m_now)

        direct_late(l)
        half = lw // 2
        slot = lax.rem(l, 2)
        for n in range(2):
            cols = pl.ds(pl.multiple_of(l * lw + n * half, half), half)
            x = jnp.dot(b_all[...], d_all[:, cols], preferred_element_type=F32)
            x = (x * inv).astype(BF16)
            stage[slot, :, n * half:(n + 1) * half] = x
        l_out(l).start()

        @pl.when(l > 0)
        def _():
            l_send(l - 1)

        @pl.when(turn)
        def _():
            forward_finish(m_now)

        return carry

    for cp in bt_load(0, 0):
        cp.start()
    lax.fori_loop(0, nl, left_step, 0)
    l_send(nl - 1)

    wacc[...] = jnp.zeros_like(wacc)

    def right_loads(m):
        srcs = (rown.at[m, target(row, 1)], rfa.at[m], rfb.at[m])
        return [
            pltpu.make_async_copy(
                src, b_all.at[n * piece:(n + 1) * piece, 7 * wide:8 * wide], rl_sem.at[n]
            )
            for n, src in enumerate(srcs)
        ]

    def right_out(m, sent=False):
        slot = lax.rem(m, 2)
        cols = pl.ds(pl.multiple_of((core * nq + m) * wide, wide), wide)

        def rows(k):
            at = slot * piece + k * quarter
            return b_all.at[pl.ds(pl.multiple_of(at, quarter), quarter), 6 * wide:7 * wide]

        away = remote(rows(1 - core), rfin.at[:, cols], rx_s.at[m], rx_r.at[m], depth=buddy)
        if sent:
            return away
        return pltpu.make_async_copy(rows(core), rfin.at[:, cols], rx_l.at[m]), away

    def right_final_start(m):
        fa_copy(m).wait_recv()
        fb_copy(m, 0).wait_recv()
        for cp in right_loads(m):
            cp.start()

    def right_final_finish(m):
        for cp in right_loads(m):
            cp.wait()

        @pl.when(m >= 2)
        def _():
            mine, theirs = right_out(m - 2)
            mine.wait()
            theirs.wait_send()

        total = sum(
            b_all[n * piece:(n + 1) * piece, 7 * wide:8 * wide].astype(F32) for n in range(3)
        ).astype(BF16)
        at = pl.multiple_of(lax.rem(m, 2) * piece, piece)
        b_all[pl.ds(at, piece), 6 * wide:7 * wide] = total
        for cp in right_out(m):
            cp.start()

    def left_loads(p):
        cps = []
        for h in range(2):
            l = 2 * p + h
            srcs = [lown.at[l, target(core * 2 + col, 1)]] + [lrecv.at[r, l] for r in range(3)]
            for n, src in enumerate(srcs):
                dst = b_all.at[n * piece:(n + 1) * piece, h * lw:(h + 1) * lw]
                cps.append(pltpu.make_async_copy(src, dst, ll_sem.at[h, n]))
        return cps

    def left_out_copy(p):
        cs = pl.ds(pl.multiple_of(p * 8, 8), 8)
        return pltpu.make_async_copy(lbuf.reshape(piece, 8, toks), left_out.at[:, cs], lo_sem.at[0])

    def left_final_start(p):
        for h in range(2):
            for r in range(3):
                l_copy(2 * p + h, r).wait_recv()
        for cp in left_loads(p):
            cp.start()

    def left_final_finish(p):
        for cp in left_loads(p):
            cp.wait()

        @pl.when(p >= 1)
        def _():
            left_out_copy(p - 1).wait()

        for h in range(2):
            for c in range(4):
                cols = slice(h * lw + c * toks, h * lw + (c + 1) * toks)
                lbuf[pl.ds(4 * h + c, piece, stride=8), :] = sum(
                    b_all[n * piece:(n + 1) * piece, cols].astype(F32) for n in range(4)
                )
        left_out_copy(p).start()

    def outer_step(o, carry):
        direct_late(nl + o)
        left_turn = o >= nq - 3
        turn = jnp.logical_and(inner, jnp.logical_or(o == 1, o == 3))
        m_now = 6 + o // 3
        p_now = jnp.maximum(o - (nq - 3), 0)

        @pl.when(turn)
        def _():
            forward_start(m_now)

        @pl.when(o < early)
        def _():
            right_final_start(o)

        @pl.when(left_turn)
        def _():
            left_final_start(p_now)

        slot = lax.rem(o, 2)
        for cp in bt_load(o, slot):
            cp.wait()

        @pl.when(o < nq - 1)
        def _():
            for cp in bt_load(o + 1, 1 - slot):
                cp.start()

        width = 512
        for n in range(a_all.shape[1] // width):
            cols = slice(n * width, (n + 1) * width)
            x = jnp.dot(btc[slot, 0], a_all[:seqs, cols], preferred_element_type=F32)
            x += jnp.dot(btc[slot, 1], a_all[seqs:, cols], preferred_element_type=F32)
            d_all[:wide, cols] = (x * inv).astype(BF16)
        right = g_all[pl.ds(pl.multiple_of(o * jq, jq), jq)].reshape(jq * toks, -1)
        cg = 8
        for c0 in range(0, chans, cg):
            left = jnp.concatenate(
                [
                    jnp.concatenate(
                        [
                            d_all[j * chans:(j + 1) * chans, c * toks:(c + 1) * toks]
                            for j in range(jq)
                        ],
                        axis=1,
                    )
                    for c in range(c0, c0 + cg)
                ],
                axis=0,
            )
            wacc[c0 * chans:(c0 + cg) * chans] += jnp.dot(left, right, preferred_element_type=F32)

        @pl.when(turn)
        def _():
            forward_finish(m_now)

        @pl.when(o < early)
        def _():
            right_final_finish(o)

        @pl.when(left_turn)
        def _():
            left_final_finish(p_now)

        return carry

    early = nq - 1
    lax.fori_loop(0, nq, outer_step, 0)

    n1 = wacc.shape[0] // n_depth
    n2 = n1 // n_row
    n3 = n2 // 2

    def part(ref, index, size):
        return ref.at[pl.ds(pl.multiple_of(index * size, size), size)]

    def w1_copy(m):
        to = lax.rem(depth + m + 1, n_depth)
        return remote(part(w1s, to, n1), w1r.at[m], w1_s.at[m], w1_q.at[m], depth=to)

    def w2_copy(m):
        to = lax.rem(row + m + 1, n_row)
        return remote(part(w2s, to, n2), w2r.at[m], w2_s.at[m], w2_q.at[m], row=to)

    w3_copy = remote(part(w3s, 1 - col, n3), w3r, w3_sem.at[0], w3_sem.at[1], col=1 - col)

    w1s[...] = wacc[...].astype(BF16)
    for m in range(n_depth - 1):
        w1_copy(m).start()
    for m in range(n_depth - 1):
        w1_copy(m).wait()
    w2s[...] = part(wacc, depth, n1)[...] + sum(w1r[m].astype(F32) for m in range(n_depth - 1))
    for m in range(n_row - 1):
        w2_copy(m).start()
    right_final_start(nq - 1)
    right_final_finish(nq - 1)
    for m in range(n_row - 1):
        w2_copy(m).wait()
    w3s[...] = part(w2s, row, n2)[...] + sum(w2r[m] for m in range(n_row - 1))
    w3_copy.start()
    left_final_start(nl // 2 - 1)
    left_final_finish(nl // 2 - 1)

    @pl.when(inner)
    def _():
        for m in (nq - 2, nq - 1):
            for u in range(2):
                fb_copy(m, u).wait_send()

    for m in (nq - 2, nq - 1):
        mine, theirs = right_out(m)
        mine.wait()
        theirs.wait_send()
    left_out_copy(nl // 2 - 1).wait()

    def drain(q, carry):
        @pl.when(q > 0)
        def _():
            for m in range(n_depth - 1):
                g_copy(m, q).wait_send()

        b_copy(q).wait_send()
        fa_copy(q).wait_send()
        right_out(q, True).wait_recv()

        @pl.when(jnp.logical_not(inner))
        def _():
            fw_copy(q).wait_send()

        return carry

    lax.fori_loop(0, nq, drain, 0)

    def drain_l(l, carry):
        for r in range(3):
            l_copy(l, r).wait_send()
        return carry

    lax.fori_loop(0, nl, drain_l, 0)
    w3_copy.wait()
    w_out[...] = part(w3s, col, n3)[...] + w3r[...]


def mega_call(a2, bt, gt, w, inv, chans, toks):
    seqs, ci = a2.shape
    jh, je = gt.shape[1], bt.shape[1]
    i_own, pair_ch = gt.shape[2:]
    n_depth, n_row = lax.axis_size("depth"), lax.axis_size("row")
    nq = nl = 8
    wide = je // nq
    lw = ci // nl
    quarter = seqs // n_row
    piece = 2 * quarter
    n1 = chans * chans // n_depth
    n2 = n1 // n_row
    n3 = n2 // 2
    hbm = lambda *s: jax.ShapeDtypeStruct(s, BF16)
    dma = lambda *s: pltpu.SemaphoreType.DMA(s)
    anyspec = pl.BlockSpec(memory_space=pl.ANY)
    vmem = pl.BlockSpec(memory_space=pltpu.VMEM)
    eye = jnp.asarray(np.eye(seqs), BF16)
    return pl.pallas_call(
        functools.partial(mega_kernel, (chans, seqs, toks, nq, nl, quarter), inv),
        out_shape=(
            hbm(nq, n_row * piece, wide),
            hbm(nq, 2 * piece, wide),
            hbm(nq, piece, wide),
            hbm(nq, piece, wide),
            hbm(nl, n_row * piece, lw),
            hbm(3, nl, piece, lw),
            hbm(je, seqs),
            hbm(quarter, 2 * je),
            jax.ShapeDtypeStruct((piece, chans, toks), F32),
            jax.ShapeDtypeStruct((n3, pair_ch), F32),
        ),
        in_specs=[anyspec, anyspec, anyspec, vmem, vmem],
        out_specs=(anyspec,) * 9 + (vmem,),
        scratch_shapes=[
            pltpu.VMEM((2 * seqs, ci), BF16),
            pltpu.VMEM((je, ci), BF16),
            pltpu.VMEM((2 * seqs, je), BF16),
            pltpu.VMEM((jh, i_own * n_depth, pair_ch), BF16),
            pltpu.VMEM((2, n_row * piece, wide), BF16),
            pltpu.VMEM((2, 2, wide, seqs), BF16),
            pltpu.VMEM((2, 2 * piece, wide), BF16),
            pltpu.VMEM((2, 2 * piece, wide), BF16),
            pltpu.VMEM((piece * 8, toks), F32),
            pltpu.VMEM((chans * chans, pair_ch), F32),
            pltpu.VMEM((chans * chans, pair_ch), BF16),
            pltpu.VMEM((n_depth - 1, n1, pair_ch), BF16),
            pltpu.VMEM((n1, pair_ch), F32),
            pltpu.VMEM((n_row - 1, n2, pair_ch), F32),
            pltpu.VMEM((n2, pair_ch), F32),
            pltpu.VMEM((n3, pair_ch), F32),
            dma(3), dma(1), dma(n_depth - 1, nq), dma(n_depth - 1, nq), dma(nq), dma(nq), dma(2),
            dma(nq), dma(nq), dma(nq), dma(nq), dma(2, nq), dma(nq),
            dma(3, nl), dma(3, nl), dma(2, 2), dma(2),
            dma(nq), dma(nq), dma(nq), dma(3), dma(2, 4), dma(1),
            dma(n_depth - 1), dma(n_depth - 1), dma(n_row - 1), dma(n_row - 1), dma(2),
        ],
        compiler_params=pltpu.CompilerParams(
            vmem_limit_bytes=MEGA_VMEM, collective_id=0, has_side_effects=True
        ),
        cost_estimate=cost(6 * seqs * 2 * je * ci, 8 * seqs * ci),
        name="mega",
    )(a2, bt, gt, w, eye)


def post_kernel(chans, l_ref, r_ref, eye_ref, l_out, r_out, tmp, mix):
    rows, je = r_ref.shape
    wide = eye_ref.shape[0]
    group, toks = r_out.shape[1:]
    l_out[...] = l_ref[...]

    @pl.when(pl.program_id(0) == 0)
    def _():
        for n in range(je // wide):
            tmp[n * wide:(n + 1) * wide, :rows] = lax.dot_general(
                eye_ref[...], r_ref[:, n * wide:(n + 1) * wide], (((1,), (1,)), ((), ())),
                preferred_element_type=F32,
            )

    first = pl.program_id(0) * group
    lanes = mix.shape[2]
    for e in range(group):
        x = tmp[pl.ds(first + e, toks, stride=chans), :][:, :rows].astype(BF16)
        y = lax.dot_general(
            eye_ref[:rows, :rows], x, (((1,), (1,)), ((), ())), preferred_element_type=F32
        )
        for k in range(mix.shape[0]):
            mix[k, pl.ds(e, rows, stride=group), :] = y[:, k * lanes:(k + 1) * lanes]
    for k in range(mix.shape[0]):
        r_out[:, :, k * lanes:(k + 1) * lanes] = mix[k].reshape(rows, group, lanes)


def post_call(left, rfin, toks):
    srows, chans, width = left.shape
    rows, je = rfin.shape
    steps = chans // 8
    return pl.pallas_call(
        functools.partial(post_kernel, chans),
        out_shape=(
            jax.ShapeDtypeStruct(left.shape, F32),
            jax.ShapeDtypeStruct((rows, chans, toks), F32),
        ),
        grid=(steps,),
        in_specs=[
            pl.BlockSpec((srows // steps, chans, width), lambda n: (n, 0, 0)),
            pl.BlockSpec((rows, je), lambda n: (0, 0)),
            pl.BlockSpec((256, 256), lambda n: (0, 0)),
        ],
        out_specs=(
            pl.BlockSpec((srows // steps, chans, width), lambda n: (n, 0, 0)),
            pl.BlockSpec((rows, 8, toks), lambda n: (0, n, 0)),
        ),
        scratch_shapes=[pltpu.VMEM((je, 128), F32), pltpu.VMEM((toks // 128, rows * 8, 128), F32)],
        compiler_params=params(),
        name="post",
    )(left, rfin, jnp.asarray(np.eye(256), BF16))


def mega_body(left_factor, right_factor, out_weight, pair_cotangent):
    seqs, chans, rows = left_factor.shape
    toks = right_factor.shape[2]
    inv = 1.0 / (seqs * lax.axis_size("depth"))
    jh = toks // 2
    a2 = left_factor.reshape(seqs, chans * rows)
    bt = jnp.transpose(right_factor, (2, 1, 0)).reshape(2, jh * chans, seqs)
    gt = jnp.transpose(pair_cotangent, (1, 0, 2)).reshape(2, jh, -1, pair_cotangent.shape[2])
    *_, rfin, left_grad, weight_grad = mega_call(a2, bt, gt, out_weight, inv, chans, rows)

    left_grad, right_grad = post_call(left_grad, rfin, toks)
    return left_grad, right_grad, weight_grad


def plain_body(left_factor, right_factor, out_weight, pair_cotangent):
    seq_total = left_factor.shape[0] * lax.axis_size("depth")
    chans = left_factor.shape[1]
    rows_here = left_factor.shape[2]
    cols_here = right_factor.shape[2]
    width = out_weight.shape[0]
    pair_ch = out_weight.shape[1]
    natural = jnp.einsum("sci,sej->ciej", left_factor, right_factor, preferred_element_type=F32) / seq_total
    outer = jnp.transpose(natural.astype(BF16), (1, 3, 0, 2)).reshape(rows_here * cols_here, width)
    piece = lax.all_gather(pair_cotangent, "depth", axis=0, tiled=True)
    grad_two = piece.reshape(rows_here * cols_here, pair_ch)
    delta = jnp.dot(grad_two, out_weight.T, preferred_element_type=F32).astype(BF16)
    weight_acc = jnp.dot(outer.T, grad_two, preferred_element_type=F32)
    delta_four = delta.reshape(rows_here, cols_here, chans, chans)
    left_part = jnp.einsum("ijce,sej->sci", delta_four, right_factor, preferred_element_type=F32) / seq_total
    right_part = jnp.einsum("ijce,sci->sej", delta_four, left_factor, preferred_element_type=F32) / seq_total
    left_grad = lax.psum_scatter(left_part, "col", scatter_dimension=0, tiled=True)
    right_grad = lax.psum_scatter(right_part, "row", scatter_dimension=0, tiled=True)
    middle = lax.psum_scatter(weight_acc, ("depth", "row"), scatter_dimension=0, tiled=True)
    weight_grad = lax.psum_scatter(middle, "col", scatter_dimension=0, tiled=True)
    return left_grad, right_grad, weight_grad


def body(left_factor, right_factor, out_weight, pair_cotangent):
    seqs, chans, rows = left_factor.shape
    toks = right_factor.shape[2]
    fits = toks % 128 == 0 and toks <= 256 and rows % 32 == 0 and chans == 32 and seqs <= 512
    shape = tuple(lax.axis_size(x) for x in ("depth", "row", "col"))
    mega = (
        fits and shape == (4, 4, 2) and toks == 256 and rows == 128 and seqs % 64 == 0
        and out_weight.shape[1] == 128
    )
    run = mega_body if mega else fused_body if fits else plain_body
    return run(left_factor, right_factor, out_weight, pair_cotangent)


def solution(mesh):
    return jax.shard_map(
        body,
        mesh=mesh,
        in_specs=(
            P("depth", None, "row"),
            P("depth", None, "col"),
            P(),
            P(("row", "depth"), "col", None),
        ),
        out_specs=(
            P(("depth", "col"), None, "row"),
            P(("depth", "row"), None, "col"),
            P(("depth", "row", "col"), None),
        ),
        check_vma=False,
    )
```
